128 devices in a mesh: var: 16 (over x_hi, z, core), tp: 8 (over y, x_lo).
Axes of the slice: x: 4 (x_hi: 2, x_lo: 2; x = x_hi * 2 + x_lo), y: 4, z: 4, core: 2. Of those that a mesh axis runs over, the one named last changes fastest.
Arguments:
- hidden_in: bfloat16 [48, 384, 2048], P('var'), may hold values from -100 to 100
- run_table: int32 [48, 2], P('var'), may hold values 0 or 1
- qkv_weight: bfloat16 [2048, 3072], P('var', 'tp'), may hold values from -1 to 1
- out_weight: bfloat16 [2048, 2048], P('tp', 'var'), may hold values from -0.125 to 0.125
- gate_up_weight: bfloat16 [2048, 2, 8192], P('var', None, 'tp'), may hold values from -0.125 to 0.125
- down_weight: bfloat16 [8192, 2048], P('tp', 'var'), may hold values from -0.0625 to 0.0625
Outputs:
- layer_out: bfloat16 [48, 384, 2048], P('var')
The draws below stay inside these ranges and needn't reach their ends.
All inputs are finite; a program needn't handle non-finite values. No bound on the sum of `run_table` on one device may be relied on, other than what follows from the above.
Results may differ from the reference program's by a relative error of at most 0.0075.
Values may be sent and summed in bfloat16 or wider, within the bound.
No kernel may reach another device: no remote copies, remote signals or barrier semaphores. Data moves between devices by JAX's collectives and lax.ppermute only.
A program may use at most 128 MiB of HBM per device.

```python
import jax
import jax.numpy as jnp
from jax import lax

D = 2048
FF = 8192
QUERY_HEADS = 32
KEY_VALUE_HEADS = 8
HEAD_SIZE = 64
PROMPT_LENGTH = 384
SEQS = 48
N_TP = 8


def draw_hidden_in(key, part):
    key_collection = jax.random.split(jax.random.fold_in(key, 11), 3)
    full_shape = (SEQS, PROMPT_LENGTH, D)
    base_field = jax.random.normal(key_collection[0], full_shape, jnp.float32)
    row_scale = jnp.exp(jax.random.uniform(key_collection[1], (SEQS, PROMPT_LENGTH, 1), jnp.float32, jnp.log(0.3), jnp.log(3.0)))
    col_scale = jnp.exp(jax.random.uniform(key_collection[2], (1, 1, D), jnp.float32, jnp.log(0.3), jnp.log(3.0)))
    drawn = base_field * row_scale * col_scale
    return jnp.clip(drawn, -100.0, 100.0).astype(jnp.bfloat16)


def draw_qkv_weight(key, part):
    key_collection = jax.random.split(jax.random.fold_in(key, 23), 1)
    query_slice = QUERY_HEADS // N_TP
    key_value_slice = KEY_VALUE_HEADS // N_TP
    block_width = (query_slice + 2 * key_value_slice) * HEAD_SIZE
    column_count = N_TP * block_width
    base_field = jax.random.normal(key_collection[0], (D, column_count), jnp.float32) * D ** (-0.5)
    return jnp.clip(base_field, -1.0, 1.0).astype(jnp.bfloat16)


def set_ends(result, own_key, least, top_value):
    longest = result.shape.index(max(result.shape))
    spots = []
    for shift in (0, 1):
        where = [jax.random.randint(jax.random.fold_in(own_key, axis), (), 0, length) for axis, length in enumerate(result.shape)]
        where[longest] = (where[longest] + shift) % result.shape[longest]
        spots.append(tuple(where))
    return result.at[spots[0]].set(least).at[spots[1]].set(top_value)


def level_of(key, shape, shards, least, high):
    factor_of, own = 1.0, jax.random.fold_in(key, 6)
    for position, parts in shards:
        heights = jnp.exp(jax.random.uniform(jax.random.fold_in(own, position), (parts,), jnp.float32, least / len(shards), high / len(shards)))
        factor_of = factor_of * jnp.repeat(heights, shape[position] // parts).reshape([-1 if axis == position else 1 for axis in range(len(shape))])
    return factor_of


def gaussian(own_key, dims, spread, most, cuts=(), kind=jnp.bfloat16):
    entries = jax.random.normal(own_key, dims, jnp.float32) * spread
    if len(cuts) > 0:
        entries = level_of(own_key, dims, cuts, -0.22, 0.18) * entries
    return jnp.clip(entries, min=-most, max=most).astype(kind)


def setup_inputs(seed: int = 0) -> dict:
    splits = jax.random.split(jax.random.key(seed), 7)
    hidden_in = draw_hidden_in(jax.random.fold_in(splits[6], 71), 0)
    run_table = set_ends((jax.random.randint(splits[1], (SEQS, 2), 0, 4) < 3).astype(jnp.int32), jax.random.fold_in(splits[1], 1), 0, 1)
    qkv_weight = draw_qkv_weight(jax.random.fold_in(splits[6], 71), 0)
    out_weight = gaussian(splits[3], (QUERY_HEADS * HEAD_SIZE, D), (QUERY_HEADS * HEAD_SIZE) ** -0.5, 0.125, ((0, 8), (1, 16)))
    gate_up_weight = gaussian(splits[4], (D, 2, FF), D ** -0.5, 0.125, ((0, 16), (2, 8)))
    down_weight = gaussian(splits[5], (FF, D), FF ** -0.5, 0.0625, ((0, 8), (1, 16)))
    return {"hidden_in": hidden_in, "run_table": run_table, "qkv_weight": qkv_weight, "out_weight": out_weight, "gate_up_weight": gate_up_weight, "down_weight": down_weight}


def rms_norm(tensor):
    widened = tensor.astype(jnp.float32)
    scaled = widened * lax.rsqrt(lax.optimization_barrier(jnp.mean(widened * widened, axis=-1, keepdims=True)) + 1e-05)
    return scaled.astype(jnp.bfloat16)

def rotary_embedding(tensor, token_positions):
    half_width = tensor.shape[-1] // 2
    exponent = jnp.arange(half_width, dtype=jnp.float32) * (2.0 / tensor.shape[-1])
    frequency = jnp.power(jnp.float32(500000.0), -exponent)
    angles = token_positions[:, None, None] * frequency[None, None, :]
    cosine = jnp.cos(angles)
    sine_part = jnp.sin(angles)
    first_half = tensor[..., :half_width]
    second_half = tensor[..., half_width:]
    return jnp.concatenate([first_half * cosine - second_half * sine_part, second_half * cosine + first_half * sine_part], axis=-1)

def block_sum(terms):
    rounded = lax.optimization_barrier(terms.astype(jnp.bfloat16))
    return lax.optimization_barrier(jnp.sum(rounded.astype(jnp.float32), axis=0))

def reference(hidden_in, run_table, qkv_weight, out_weight, gate_up_weight, down_weight):
    query_slice = QUERY_HEADS // N_TP
    key_value_slice = KEY_VALUE_HEADS // N_TP
    group_width = QUERY_HEADS // KEY_VALUE_HEADS
    ff_local = FF // N_TP
    out_blocks = out_weight.astype(jnp.float32).reshape(N_TP, query_slice * HEAD_SIZE, D)
    down_blocks = down_weight.astype(jnp.float32).reshape(N_TP, ff_local, D)
    gate_up_flat = gate_up_weight.reshape(D, 2 * FF)

    def one_sequence(packed):
        sequence, switches = packed
        switches = switches.astype(jnp.float32)
        normed = rms_norm(sequence)
        projected_rows = jnp.dot(normed, qkv_weight, preferred_element_type=jnp.float32)
        projected_rows = projected_rows.reshape(PROMPT_LENGTH, N_TP, query_slice + 2 * key_value_slice, HEAD_SIZE)
        token_positions = jnp.arange(PROMPT_LENGTH, dtype=jnp.float32)
        query_rows = rotary_embedding(projected_rows[:, :, :query_slice].reshape(PROMPT_LENGTH, QUERY_HEADS, HEAD_SIZE), token_positions).astype(jnp.bfloat16)
        keys_bfloat = rotary_embedding(projected_rows[:, :, query_slice:query_slice + key_value_slice].reshape(PROMPT_LENGTH, KEY_VALUE_HEADS, HEAD_SIZE), token_positions).astype(jnp.bfloat16)
        values_bfloat = projected_rows[:, :, query_slice + key_value_slice:].reshape(PROMPT_LENGTH, KEY_VALUE_HEADS, HEAD_SIZE).astype(jnp.bfloat16)
        grouped_queries = query_rows.reshape(PROMPT_LENGTH, KEY_VALUE_HEADS, group_width, HEAD_SIZE).astype(jnp.float32)
        scores = jnp.einsum('qkgd,pkd->kgqp', grouped_queries, keys_bfloat.astype(jnp.float32)) * HEAD_SIZE ** (-0.5)
        causal = jnp.arange(PROMPT_LENGTH)[:, None] >= jnp.arange(PROMPT_LENGTH)[None, :]
        scores = jnp.where(causal, scores, jnp.float32(-1e+30))
        row_max = lax.optimization_barrier(jnp.max(scores, axis=-1, keepdims=True))
        exped = jnp.exp(scores - row_max)
        weights_bf = (exped / lax.optimization_barrier(jnp.sum(exped, axis=-1, keepdims=True))).astype(jnp.bfloat16)
        head_outputs = jnp.einsum('kgqp,pkd->qkgd', weights_bf.astype(jnp.float32), values_bfloat.astype(jnp.float32))
        head_outputs = head_outputs.astype(jnp.bfloat16).reshape(PROMPT_LENGTH, N_TP, query_slice * HEAD_SIZE)
        attn_terms = jnp.einsum('sjc,jcd->jsd', head_outputs.astype(jnp.float32), out_blocks)
        attention = block_sum(attn_terms)
        after_attention = (sequence.astype(jnp.float32) + switches[0] * attention).astype(jnp.bfloat16)
        normed_two = rms_norm(after_attention)
        gate_and_up = jnp.dot(normed_two, gate_up_flat, preferred_element_type=jnp.float32)
        hidden = (jax.nn.silu(gate_and_up[:, :FF]) * gate_and_up[:, FF:]).astype(jnp.bfloat16)
        mlp_terms = jnp.einsum('sjc,jcd->jsd', hidden.reshape(PROMPT_LENGTH, N_TP, ff_local).astype(jnp.float32), down_blocks)
        mlp = block_sum(mlp_terms)
        return (after_attention.astype(jnp.float32) + switches[1] * mlp).astype(jnp.bfloat16)
    return lax.map(one_sequence, (hidden_in, run_table))
```

```python
import jax
import jax.numpy as jnp
from jax import lax
from jax.experimental import pallas as pl
from jax.experimental.pallas import tpu as pltpu
from jax.sharding import PartitionSpec as P

QUERY_HEADS = 32
KEY_VALUE_HEADS = 8
HEAD_SIZE = 64
BF = jnp.bfloat16
F32 = jnp.float32

VAR_XH = [(v, v ^ 8) for v in range(16)]
VAR_CORE = [(v, v ^ 1) for v in range(16)]
TP_XL = [(t, t ^ 1) for t in range(8)]
ORDER = [(0, 0), (0, 1), (1, 0), (1, 1), (3, 0), (3, 1), (2, 0), (2, 1)]


def var_z(step):
    return [(v, (v & 9) | ((((v >> 1) & 3) + step) % 4) << 1) for v in range(16)]


def tp_y(step):
    return [(t, (t & 1) | (((t >> 1) + step) % 4) << 1) for t in range(8)]


VAR = ("var", VAR_XH, var_z(1), var_z(3))
TP = ("tp", TP_XL, tp_y(1), tp_y(3))


def halves(pair, axis):
    return lax.split(pair, [pair.shape[axis] // 2] * 2, axis=axis)


def gather_eight(piece, axis, group):
    name, flip, up, down = group
    own = jnp.concatenate([piece, lax.ppermute(piece, name, flip)], axis=axis)
    back = lax.ppermute(own, name, up)
    ahead = lax.ppermute(own, name, down)
    far = [
        lax.ppermute(halves(back, axis)[0], name, up),
        lax.ppermute(halves(ahead, axis)[1], name, down),
    ]
    return [own, back, ahead] + far


def gather_half(piece, axis, group):
    return jnp.concatenate(gather_eight(piece, axis, group), axis=axis)


def rms_norm(tensor):
    widened = tensor.astype(F32)
    scaled = widened * lax.rsqrt(jnp.mean(widened * widened, axis=-1, keepdims=True) + 1e-05)
    return scaled.astype(BF)


def move_blocks_kernel(order_ref, in_ref, out_ref):
    out_ref[...] = in_ref[...]


def move_blocks(tensor, order):
    rows, columns = tensor.shape
    return pl.pallas_call(
        move_blocks_kernel,
        out_shape=jax.ShapeDtypeStruct(tensor.shape, tensor.dtype),
        grid_spec=pltpu.PrefetchScalarGridSpec(
            num_scalar_prefetch=1,
            grid=(16,),
            in_specs=[pl.BlockSpec((rows, 128), lambda j, order_ref: (0, order_ref[j]))],
            out_specs=pl.BlockSpec((rows, 128), lambda j, order_ref: (0, j)),
        ),
    )(order, tensor)


def rotary_embedding(tensor, token_positions):
    half_width = tensor.shape[-1] // 2
    exponent = jnp.arange(half_width, dtype=F32) * (2.0 / tensor.shape[-1])
    frequency = jnp.power(F32(500000.0), -exponent)
    angles = token_positions[:, None, None] * frequency[None, None, :]
    cosine = jnp.cos(angles)
    sine_part = jnp.sin(angles)
    first_half = tensor[..., :half_width]
    second_half = tensor[..., half_width:]
    return jnp.concatenate(
        [
            first_half * cosine - second_half * sine_part,
            second_half * cosine + first_half * sine_part,
        ],
        axis=-1,
    )


def attend(query_rows, keys_bfloat, values_bfloat, score_scale):
    scores = (
        jnp.einsum("bqkgd,bpkd->bkgqp", query_rows, keys_bfloat, preferred_element_type=F32)
        * score_scale
    )
    length = scores.shape[-1]
    causal = jnp.arange(length)[:, None] >= jnp.arange(length)[None, :]
    scores = jnp.where(causal, scores, F32(-1e30))
    row_max = jnp.max(scores, axis=-1, keepdims=True)
    exped = jnp.exp(scores - row_max)
    weights_bf = (exped / jnp.sum(exped, axis=-1, keepdims=True)).astype(BF)
    head_outputs = jnp.einsum(
        "bkgqp,bpkd->bqkgd", weights_bf, values_bfloat, preferred_element_type=F32
    )
    return head_outputs.astype(BF)


def dot(a, b):
    return jnp.dot(a, b, preferred_element_type=F32)


def shards(hidden_in, run_table, qkv_weight, out_weight, gate_up_weight, down_weight):
    tp_count = lax.axis_size("tp")
    seq_count, full_len, model_width = hidden_in.shape
    row_count = seq_count * full_len
    own_rows = row_count // tp_count
    query_slice = QUERY_HEADS // tp_count
    key_value_slice = KEY_VALUE_HEADS // tp_count
    group_width = QUERY_HEADS // KEY_VALUE_HEADS
    var_index = lax.axis_index("var")
    tp_index = lax.axis_index("tp")
    half = model_width // 2

    x_hi, z_at, core = var_index // 8, (var_index // 2) % 4, var_index % 2
    block_of = jnp.stack(
        [
            (x_hi ^ pair) * 8 + ((z_at - back) % 4) * 2 + (core ^ other)
            for other in range(2)
            for back, pair in ORDER
        ]
    ).astype(jnp.int32)
    place_of = jnp.argsort(block_of).astype(jnp.int32)
    y_at, x_lo = tp_index // 2, tp_index % 2
    source_of = [((y_at - back) % 4) * 2 + (x_lo ^ pair) for back, pair in ORDER]

    def from_partner(tensor):
        return lax.ppermute(tensor, "var", VAR_CORE)

    qkv_one = gather_half(qkv_weight, 0, VAR)
    qkv_two = from_partner(qkv_one)
    out_block = gather_half(out_weight, 1, VAR)
    out_one = gather_half(out_block, 0, TP)
    out_two = from_partner(out_one)
    ff_local = gate_up_weight.shape[2]
    gate_up_one = gather_half(gate_up_weight.reshape(-1, 2 * ff_local), 0, VAR)
    gate_up_two = from_partner(gate_up_one)
    down_one = gather_half(down_weight, 1, VAR)
    down_two = from_partner(down_one)

    flat_hidden = hidden_in.reshape(row_count, model_width)
    columns = move_blocks(rms_norm(flat_hidden), block_of)
    projected_rows = dot(columns[:, :half], qkv_one) + dot(columns[:, half:], qkv_two)
    projected_rows = projected_rows.reshape(
        seq_count, full_len, query_slice + 2 * key_value_slice, HEAD_SIZE
    )
    token_positions = jnp.arange(full_len, dtype=F32)
    query_rows = rotary_embedding(projected_rows[:, :, :query_slice], token_positions).astype(BF)
    query_rows = query_rows.reshape(seq_count, full_len, key_value_slice, group_width, HEAD_SIZE)
    keys_bfloat = rotary_embedding(
        projected_rows[:, :, query_slice : query_slice + key_value_slice], token_positions
    ).astype(BF)
    values_bfloat = projected_rows[:, :, query_slice + key_value_slice :].astype(BF)
    head_outputs = attend(query_rows, keys_bfloat, values_bfloat, HEAD_SIZE ** (-0.5))
    head_rows = head_outputs.reshape(tp_count, own_rows, query_slice * HEAD_SIZE)

    heads = lax.all_to_all(head_rows, "tp", split_axis=0, concat_axis=0, tiled=True)
    heads = jnp.concatenate(
        [lax.dynamic_index_in_dim(heads, source, 0, keepdims=False) for source in source_of], axis=1
    )
    own_hidden = lax.dynamic_index_in_dim(
        flat_hidden.reshape(tp_count, own_rows, model_width), tp_index, 0, keepdims=False
    )
    own_hidden = move_blocks(own_hidden, block_of).astype(F32)
    switches = jnp.repeat(run_table.astype(F32), full_len, axis=0)
    switches = lax.dynamic_slice_in_dim(switches, tp_index * own_rows, own_rows, 0)
    attention = jnp.concatenate([dot(heads, out_one), dot(heads, out_two)], axis=1)
    after = (own_hidden + switches[:, :1] * attention).astype(BF)
    normed_two = rms_norm(after)

    def feed_forward(rows):
        gate_and_up = dot(rows[:, :half], gate_up_one) + dot(rows[:, half:], gate_up_two)
        hidden = (jax.nn.silu(gate_and_up[:, :ff_local]) * gate_and_up[:, ff_local:]).astype(BF)
        return jnp.concatenate(
            [dot(hidden, down_one).astype(BF), dot(hidden, down_two).astype(BF)], axis=1
        )

    own, back, ahead, far_one, far_two = gather_eight(normed_two, 0, TP)
    for_back = feed_forward(back)
    for_ahead = feed_forward(ahead)
    for_far = feed_forward(jnp.concatenate([far_one, far_two], axis=0))
    for_own = feed_forward(own)
    terms = [
        lax.ppermute(for_back, "tp", tp_y(3)),
        lax.ppermute(for_ahead, "tp", tp_y(1)),
        lax.ppermute(for_far, "tp", tp_y(2)),
    ]
    total = for_own.astype(F32)
    for term in terms:
        total = total + term.astype(F32)
    kept, given = halves(total, 0)
    mlp = kept + lax.ppermute(given.astype(BF), "tp", TP_XL).astype(F32)
    result = (after.astype(F32) + switches[:, 1:] * mlp).astype(BF)
    result = move_blocks(result, place_of)

    own, back, ahead, far_one, far_two = gather_eight(result, 0, TP)
    pieces = halves(own, 0) + halves(back, 0) + halves(ahead, 0) + [far_one, far_two]
    gathered = jnp.zeros((tp_count, own_rows, model_width), BF)
    for source, piece in zip(source_of, pieces):
        gathered = lax.dynamic_update_index_in_dim(gathered, piece, source, 0)
    return gathered.reshape(seq_count, full_len, model_width)


def solution(mesh):
    return jax.shard_map(
        shards,
        mesh=mesh,
        in_specs=(
            P("var", None, None),
            P("var", None),
            P("var", "tp"),
            P("tp", "var"),
            P("var", None, "tp"),
            P("tp", "var"),
        ),
        out_specs=P("var", None, None),
        check_vma=False,
    )
```

```python
import functools

import jax
import jax.numpy as jnp
from jax import lax
from jax.experimental import pallas as pl
from jax.experimental.pallas import tpu as pltpu
from jax.sharding import PartitionSpec as P

QUERY_HEADS = 32
KEY_VALUE_HEADS = 8
HEAD_SIZE = 64
BF = jnp.bfloat16
F32 = jnp.float32

VAR_XH = [(v, v ^ 8) for v in range(16)]
VAR_CORE = [(v, v ^ 1) for v in range(16)]
TP_XL = [(t, t ^ 1) for t in range(8)]
PAIR_FIRST = [(0, 0), (0, 1), (1, 0), (1, 1), (3, 0), (3, 1), (2, 0), (2, 1)]
RING_FIRST = [(0, 0), (1, 0), (3, 0), (2, 0), (0, 1), (1, 1), (3, 1), (2, 1)]
LANES = 128


def var_z(step):
    return [(v, (v & 9) | ((((v >> 1) & 3) + step) % 4) << 1) for v in range(16)]


def tp_y(step):
    return [(t, (t & 1) | (((t >> 1) + step) % 4) << 1) for t in range(8)]


VAR = ("var", VAR_XH, var_z(1), var_z(3))
TP = ("tp", TP_XL, tp_y(1), tp_y(3))


def halves(pair, axis):
    return lax.split(pair, [pair.shape[axis] // 2] * 2, axis=axis)


def gather_pair_first(piece, axis, group):
    name, flip, up, down = group
    own = jnp.concatenate([piece, lax.ppermute(piece, name, flip)], axis=axis)
    back = lax.ppermute(own, name, up)
    ahead = lax.ppermute(own, name, down)
    far = [
        lax.ppermute(halves(back, axis)[0], name, up),
        lax.ppermute(halves(ahead, axis)[1], name, down),
    ]
    return [own, back, ahead] + far


def gather_ring_first(piece, axis, group):
    name, flip, up, down = group
    back = lax.ppermute(piece, name, up)
    ahead = lax.ppermute(piece, name, down)
    far = [
        lax.ppermute(halves(back, axis)[0], name, up),
        lax.ppermute(halves(ahead, axis)[1], name, down),
    ]
    ring = [piece, back, ahead] + far
    return ring, lax.ppermute(jnp.concatenate(ring, axis=axis), name, flip)


def gather_half(piece, axis, group):
    return jnp.concatenate(gather_pair_first(piece, axis, group), axis=axis)


def compiler_params(mib):
    return pltpu.CompilerParams(vmem_limit_bytes=mib * 2**20)


def dot(a, b):
    return jnp.dot(a, b, preferred_element_type=F32)


def lanes(block):
    return pl.ds(pl.multiple_of(block * LANES, LANES), LANES)


def norm_scale(widened):
    return lax.rsqrt(jnp.mean(widened * widened, axis=-1, keepdims=True) + 1e-05)


def normed_blocks_kernel(place_ref, in_ref, out_ref):
    scale = norm_scale(in_ref[...].astype(F32))
    for j in range(16):
        block = in_ref[:, lanes(place_ref[j])].astype(F32)
        out_ref[:, j * LANES : (j + 1) * LANES] = (block * scale).astype(BF)


def normed_blocks(place, tensor):
    rows, columns = tensor.shape
    step = 128
    return pl.pallas_call(
        normed_blocks_kernel,
        out_shape=jax.ShapeDtypeStruct(tensor.shape, BF),
        grid_spec=pltpu.PrefetchScalarGridSpec(
            num_scalar_prefetch=1,
            grid=(rows // step,),
            in_specs=[pl.BlockSpec((step, columns), lambda i, place_ref: (i, 0))],
            out_specs=pl.BlockSpec((step, columns), lambda i, place_ref: (i, 0)),
        ),
        compiler_params=compiler_params(16),
        cost_estimate=pl.CostEstimate(
            flops=4 * rows * columns, bytes_accessed=4 * rows * columns, transcendentals=rows
        ),
        name="normed_blocks",
    )(place, tensor)


def row_switch(run_ref, column, first_row, rows, full_len, seq_count):
    row = first_row + lax.broadcasted_iota(jnp.int32, (rows, 1), 0)
    switch = jnp.zeros((rows, 1), F32)
    for s in range(seq_count):
        inside = (row >= s * full_len) & (row < (s + 1) * full_len)
        switch = jnp.where(inside, run_ref[2 * s + column].astype(F32), switch)
    return switch


def project_kernel(full_len, place_ref, run_ref, tp_ref, heads_ref, *refs):
    weight_refs, hidden_ref, after_ref, normed_ref, total = refs[:4], *refs[4:]
    step = pl.program_id(0)
    rows, columns = hidden_ref.shape
    width = heads_ref.shape[2]
    part = columns // 4

    @pl.when(step == 0)
    def _():
        total[...] = jnp.zeros_like(total)

    for q, weight_ref in enumerate(weight_refs):
        table = 16 + 8 * (q % 2)
        term = None
        for i in range(2):
            source = place_ref[table + 2 * step + i]
            product = dot(heads_ref[source], weight_ref[i * width : (i + 1) * width, :])
            term = product if term is None else term + product
        total[:, q * part : (q + 1) * part] += term

    @pl.when(step == 3)
    def _():
        switch = row_switch(run_ref, 0, tp_ref[0] * rows, rows, full_len, run_ref.shape[0] // 2)
        for j in range(16):
            at = slice(j * LANES, (j + 1) * LANES)
            residual = hidden_ref[:, lanes(place_ref[j])].astype(F32)
            after_ref[:, at] = (residual + switch * total[:, at]).astype(BF)
        widened = after_ref[...].astype(F32)
        normed_ref[...] = (widened * norm_scale(widened)).astype(BF)


def project(place, run_flat, tp_flat, heads, weights, flat_hidden, full_len):
    count, rows, width = heads.shape
    columns = flat_hidden.shape[1]
    depth = count * width
    whole = lambda k, *refs: (0, 0, 0)
    return pl.pallas_call(
        functools.partial(project_kernel, full_len),
        out_shape=[jax.ShapeDtypeStruct((rows, columns), BF)] * 2,
        grid_spec=pltpu.PrefetchScalarGridSpec(
            num_scalar_prefetch=3,
            grid=(4,),
            in_specs=[pl.BlockSpec((count, rows, width), whole)]
            + [pl.BlockSpec((depth // 4, columns // 4), lambda k, *refs: (k, 0))] * 4
            + [pl.BlockSpec((rows, columns), lambda k, place, run, tp: (tp[0], 0))],
            out_specs=[pl.BlockSpec((rows, columns), lambda k, *refs: (0, 0))] * 2,
            scratch_shapes=[pltpu.VMEM((rows, columns), F32)],
        ),
        compiler_params=compiler_params(24),
        cost_estimate=pl.CostEstimate(
            flops=2 * rows * depth * columns, bytes_accessed=2 * depth * columns, transcendentals=0
        ),
        name="project",
    )(place, run_flat, tp_flat, heads, *weights, flat_hidden)


def feed_forward_kernel(n_in, outs, gate_one, up_one, gate_two, up_two, down_one, down_two, *refs):
    in_refs, out_refs, rows_ref, total = refs[:n_in], refs[n_in:-2], refs[-2], refs[-1]
    step = pl.program_id(0)

    @pl.when(step == 0)
    def _():
        at = 0
        for ref in in_refs:
            rows_ref[at : at + ref.shape[0], :] = ref[...]
            at += ref.shape[0]
        total[...] = jnp.zeros_like(total)

    half = gate_one.shape[0]
    one, two = rows_ref[:, :half], rows_ref[:, half:]
    gate = dot(one, gate_one[...]) + dot(two, gate_two[...])
    up = dot(one, up_one[...]) + dot(two, up_two[...])
    hidden = (gate / (1.0 + jnp.exp(-gate)) * up).astype(BF)
    total[:, :half] += dot(hidden, down_one[...])
    total[:, half:] += dot(hidden, down_two[...])

    @pl.when(step == pl.num_programs(0) - 1)
    def _():
        at = 0
        for ref in out_refs:
            ref[...] = total[at : at + ref.shape[0], :].astype(BF)
            at += ref.shape[0]


def feed_forward(pieces, outs, gate_up_one, gate_up_two, down_one, down_two):
    half, double = gate_up_one.shape
    ff, columns = double // 2, 2 * half
    rows = sum(piece.shape[0] for piece in pieces)
    width = 256
    steps = ff // width
    whole = lambda j: (0, 0)
    gate = pl.BlockSpec((half, width), lambda j: (0, j))
    up = pl.BlockSpec((half, width), lambda j: (0, j + steps))
    down = pl.BlockSpec((width, half), lambda j: (j, 0))
    return pl.pallas_call(
        functools.partial(feed_forward_kernel, len(pieces), outs),
        out_shape=[jax.ShapeDtypeStruct((n, columns), BF) for n in outs],
        grid=(steps,),
        in_specs=[gate, up, gate, up, down, down]
        + [pl.BlockSpec(piece.shape, whole) for piece in pieces],
        out_specs=[pl.BlockSpec((n, columns), whole) for n in outs],
        scratch_shapes=[pltpu.VMEM((rows, columns), BF), pltpu.VMEM((rows, columns), F32)],
        compiler_params=compiler_params(32),
        cost_estimate=pl.CostEstimate(
            flops=6 * rows * columns * ff,
            bytes_accessed=6 * columns * ff + 4 * rows * columns,
            transcendentals=rows * ff,
        ),
        name="feed_forward",
    )(gate_up_one, gate_up_one, gate_up_two, gate_up_two, down_one, down_two, *pieces)


def finish_kernel(full_len, first, place_ref, run_ref, tp_ref, after_ref, *refs):
    term_refs, out_ref = refs[:-1], refs[-1]
    rows = out_ref.shape[0]
    own_rows = after_ref.shape[0]
    first_row = tp_ref[0] * own_rows + first
    switch = row_switch(run_ref, 1, first_row, rows, full_len, run_ref.shape[0] // 2)
    for j in range(16):
        at = slice(j * LANES, (j + 1) * LANES)
        total = term_refs[0][:, at].astype(F32)
        for ref in term_refs[1:]:
            total = total + ref[:, at].astype(F32)
        residual = after_ref[first : first + rows, at].astype(F32)
        out_ref[:, lanes(place_ref[j])] = (residual + switch * total).astype(BF)


def finish(place, run_flat, tp_flat, after, first, rows, terms, full_len):
    own_rows, columns = after.shape
    block = lambda i, *refs: (0, 0)
    return pl.pallas_call(
        functools.partial(finish_kernel, full_len, first),
        out_shape=jax.ShapeDtypeStruct((rows, columns), BF),
        grid_spec=pltpu.PrefetchScalarGridSpec(
            num_scalar_prefetch=3,
            grid=(1,),
            in_specs=[pl.BlockSpec(after.shape, block)]
            + [pl.BlockSpec((rows, columns), block)] * len(terms),
            out_specs=pl.BlockSpec((rows, columns), block),
        ),
        compiler_params=compiler_params(16),
        cost_estimate=pl.CostEstimate(
            flops=8 * rows * columns, bytes_accessed=12 * rows * columns, transcendentals=0
        ),
        name="finish",
    )(place, run_flat, tp_flat, after, *terms)


def places(var_index, tp_index):
    table = PAIR_FIRST + PAIR_FIRST + PAIR_FIRST + RING_FIRST
    back = jnp.array([b for b, _ in table], jnp.int32)
    pair = jnp.array([p for _, p in table], jnp.int32)
    item = jnp.arange(32, dtype=jnp.int32)
    other = (item // 8) % 2
    blocks = ((var_index // 8) ^ pair) * 8 + (((var_index // 2) - back) & 3) * 2
    blocks = blocks + ((var_index % 2) ^ other)
    sources = (((tp_index // 2) - back) & 3) * 2 + ((tp_index % 2) ^ pair)
    return jnp.where(item < 16, blocks, sources).astype(jnp.int32)


def rotary_embedding(tensor, token_positions):
    half_width = tensor.shape[-1] // 2
    exponent = jnp.arange(half_width, dtype=F32) * (2.0 / tensor.shape[-1])
    frequency = jnp.power(F32(500000.0), -exponent)
    angles = token_positions[:, None, None] * frequency[None, None, :]
    cosine = jnp.cos(angles)
    sine_part = jnp.sin(angles)
    first_half = tensor[..., :half_width]
    second_half = tensor[..., half_width:]
    return jnp.concatenate(
        [
            first_half * cosine - second_half * sine_part,
            second_half * cosine + first_half * sine_part,
        ],
        axis=-1,
    )


def attend(query_rows, keys_bfloat, values_bfloat, score_scale):
    scores = (
        jnp.einsum("bqkgd,bpkd->bkgqp", query_rows, keys_bfloat, preferred_element_type=F32)
        * score_scale
    )
    length = scores.shape[-1]
    causal = jnp.arange(length)[:, None] >= jnp.arange(length)[None, :]
    scores = jnp.where(causal, scores, F32(-1e30))
    row_max = jnp.max(scores, axis=-1, keepdims=True)
    exped = jnp.exp(scores - row_max)
    weights_bf = (exped / jnp.sum(exped, axis=-1, keepdims=True)).astype(BF)
    head_outputs = jnp.einsum(
        "bkgqp,bpkd->bqkgd", weights_bf, values_bfloat, preferred_element_type=F32
    )
    return head_outputs.astype(BF)


def after(value, *earlier):
    return lax.optimization_barrier((value,) + earlier)[0]


def shards(hidden_in, run_table, qkv_weight, out_weight, gate_up_weight, down_weight):
    tp_count = lax.axis_size("tp")
    seq_count, full_len, model_width = hidden_in.shape
    row_count = seq_count * full_len
    own_rows = row_count // tp_count
    query_slice = QUERY_HEADS // tp_count
    key_value_slice = KEY_VALUE_HEADS // tp_count
    group_width = QUERY_HEADS // KEY_VALUE_HEADS
    tp_index = lax.axis_index("tp")
    half = model_width // 2
    place = places(lax.axis_index("var"), tp_index)
    tp_flat = tp_index.astype(jnp.int32).reshape(1)
    run_flat = run_table.reshape(-1)

    def from_partner(tensor):
        return lax.ppermute(tensor, "var", VAR_CORE)

    qkv_pieces = gather_pair_first(qkv_weight, 0, VAR)
    qkv_one = jnp.concatenate(qkv_pieces, axis=0)
    qkv_two = from_partner(qkv_one)
    out_block = gather_half(after(out_weight, qkv_pieces[0]), 1, VAR)
    out_a = gather_half(out_block[:, : half // 2], 0, TP)
    ring, crossed = gather_ring_first(out_block[:, half // 2 :], 0, TP)
    out_b = jnp.concatenate(ring + [crossed], axis=0)
    out_weights = [out_a, out_b, from_partner(out_a), from_partner(out_b)]
    ff_local = gate_up_weight.shape[2]
    gate_up = after(gate_up_weight.reshape(-1, 2 * ff_local), qkv_pieces[1], qkv_pieces[2])
    gate_up_one = gather_half(gate_up, 0, VAR)
    gate_up_two = from_partner(gate_up_one)
    down_one = gather_half(after(down_weight, qkv_pieces[3], qkv_pieces[4]), 1, VAR)
    down_two = from_partner(down_one)

    flat_hidden = hidden_in.reshape(row_count, model_width)
    columns = normed_blocks(place, flat_hidden)
    projected_rows = dot(columns[:, :half], qkv_one) + dot(columns[:, half:], qkv_two)
    projected_rows = projected_rows.reshape(
        seq_count, full_len, query_slice + 2 * key_value_slice, HEAD_SIZE
    )
    token_positions = jnp.arange(full_len, dtype=F32)
    query_rows = rotary_embedding(projected_rows[:, :, :query_slice], token_positions).astype(BF)
    query_rows = query_rows.reshape(seq_count, full_len, key_value_slice, group_width, HEAD_SIZE)
    keys_bfloat = rotary_embedding(
        projected_rows[:, :, query_slice : query_slice + key_value_slice], token_positions
    ).astype(BF)
    values_bfloat = projected_rows[:, :, query_slice + key_value_slice :].astype(BF)
    head_outputs = attend(query_rows, keys_bfloat, values_bfloat, HEAD_SIZE ** (-0.5))
    head_rows = head_outputs.reshape(tp_count, own_rows, query_slice * HEAD_SIZE)

    heads = lax.all_to_all(head_rows, "tp", split_axis=0, concat_axis=0, tiled=True)
    after_attention, normed_two = project(
        place, run_flat, tp_flat, heads, out_weights, flat_hidden, full_len
    )

    split = 80
    rest = own_rows - split
    weights = (gate_up_one, gate_up_two, down_one, down_two)
    own_a, back_a, ahead_a, far_a, far_a2 = gather_pair_first(normed_two[:split], 0, TP)
    (own_b, back_b, ahead_b, far_b, far_b2), cross_b = gather_ring_first(normed_two[split:], 0, TP)
    for_own_a, for_own_b, for_back_b, for_ahead_b = feed_forward(
        [own_a, own_b, back_b, ahead_b], [2 * split, rest, rest, rest], *weights
    )
    for_back_a, for_ahead_a, for_far_b = feed_forward(
        [back_a, ahead_a, far_b, far_b2], [2 * split, 2 * split, rest], *weights
    )
    for_far_a, for_cross_b = feed_forward(
        [far_a, far_a2, cross_b], [2 * split, 4 * rest], *weights
    )

    terms_a = [
        for_own_a,
        lax.ppermute(for_back_a, "tp", tp_y(3)),
        lax.ppermute(for_ahead_a, "tp", tp_y(1)),
        lax.ppermute(for_far_a, "tp", tp_y(2)),
    ]
    given = sum(term[split:].astype(F32) for term in terms_a).astype(BF)
    terms_a.append(lax.ppermute(given, "tp", TP_XL))
    result_a = finish(
        place, run_flat, tp_flat, after_attention, 0, split, terms_a, full_len
    )
    crossed = lax.ppermute(for_cross_b, "tp", TP_XL)

    def joined(term, k):
        part = crossed[k * rest : (k + 1) * rest]
        return (term.astype(F32) + part.astype(F32)).astype(BF)

    terms_b = [
        for_own_b,
        crossed,
        lax.ppermute(joined(for_back_b, 1), "tp", tp_y(3)),
        lax.ppermute(joined(for_ahead_b, 2), "tp", tp_y(1)),
        lax.ppermute(joined(for_far_b, 3), "tp", tp_y(2)),
    ]
    result_b = finish(
        place, run_flat, tp_flat, after_attention, split, rest, terms_b, full_len
    )

    own, back, ahead, far, far2 = gather_pair_first(result_a, 0, TP)
    pieces_a = halves(own, 0) + halves(back, 0) + halves(ahead, 0) + [far, far2]
    ring, cross = gather_ring_first(result_b, 0, TP)
    pieces_b = ring[:3] + [jnp.concatenate(ring[3:], axis=0)]
    pieces_b = pieces_b + lax.split(cross, [rest] * 4, axis=0)
    gathered = jnp.zeros((tp_count, own_rows, model_width), BF)
    for k, piece in enumerate(pieces_a):
        gathered = lax.dynamic_update_slice(gathered, piece[None], (place[16 + k], 0, 0))
    for k, piece in enumerate(pieces_b):
        gathered = lax.dynamic_update_slice(gathered, piece[None], (place[24 + k], split, 0))
    return gathered.reshape(seq_count, full_len, model_width)


def solution(mesh):
    return jax.shard_map(
        shards,
        mesh=mesh,
        in_specs=(
            P("var", None, None),
            P("var", None),
            P("var", "tp"),
            P("tp", "var"),
            P("var", None, "tp"),
            P("tp", "var"),
        ),
        out_specs=P("var", None, None),
        check_vma=False,
    )
```

```python
import functools

import jax
import jax.numpy as jnp
from jax import lax
from jax.experimental import pallas as pl
from jax.experimental.pallas import tpu as pltpu
from jax.sharding import PartitionSpec as P


QUERY_HEADS = 32
HEAD_SIZE = 64
BF = jnp.bfloat16
F32 = jnp.float32

VAR_XH = [(v, v ^ 8) for v in range(16)]
VAR_CORE = [(v, v ^ 1) for v in range(16)]
TP_XL = [(t, t ^ 1) for t in range(8)]
PAIR_FIRST = [(0, 0), (0, 1), (1, 0), (1, 1), (3, 0), (3, 1), (2, 0), (2, 1)]
RING_FIRST = [(0, 0), (1, 0), (3, 0), (2, 0), (0, 1), (1, 1), (3, 1), (2, 1)]
LANES = 128


def var_z(step):
    return [(v, (v & 9) | ((((v >> 1) & 3) + step) % 4) << 1) for v in range(16)]


def tp_y(step):
    return [(t, (t & 1) | (((t >> 1) + step) % 4) << 1) for t in range(8)]


VAR = ("var", VAR_XH, var_z(1), var_z(3))
TP = ("tp", TP_XL, tp_y(1), tp_y(3))


def halves(pair, axis):
    return lax.split(pair, [pair.shape[axis] // 2] * 2, axis=axis)


def gather_pair_first(piece, axis, group):
    name, flip, up, down = group
    own = jnp.concatenate([piece, lax.ppermute(piece, name, flip)], axis=axis)
    back = lax.ppermute(own, name, up)
    ahead = lax.ppermute(own, name, down)
    far = [
        lax.ppermute(halves(back, axis)[0], name, up),
        lax.ppermute(halves(ahead, axis)[1], name, down),
    ]
    return [own, back, ahead] + far


def gather_ring(piece, axis, group):
    name, _, up, down = group
    back = lax.ppermute(piece, name, up)
    ahead = lax.ppermute(piece, name, down)
    far = [
        lax.ppermute(halves(back, axis)[0], name, up),
        lax.ppermute(halves(ahead, axis)[1], name, down),
    ]
    return [piece, back, ahead] + far


def cross_each(pieces, group):
    return [lax.ppermute(piece, group[0], group[1]) for piece in pieces]


def gather_half(piece, axis, group):
    return jnp.concatenate(gather_pair_first(piece, axis, group), axis=axis)


def compiler_params(mib):
    return pltpu.CompilerParams(vmem_limit_bytes=mib * 2**20)


def dot(a, b):
    return jnp.dot(a, b, preferred_element_type=F32)


def lanes(block):
    return pl.ds(pl.multiple_of(block * LANES, LANES), LANES)


def norm_scale(widened):
    return lax.rsqrt(jnp.mean(widened * widened, axis=-1, keepdims=True) + 1e-05)


def normed_blocks_kernel(place_ref, in_ref, out_ref):
    scale = norm_scale(in_ref[...].astype(F32))
    for j in range(16):
        block = in_ref[:, lanes(place_ref[j])].astype(F32)
        out_ref[:, j * LANES : (j + 1) * LANES] = (block * scale).astype(BF)


def normed_blocks(place, tensor):
    rows, columns = tensor.shape
    step = 128
    return pl.pallas_call(
        normed_blocks_kernel,
        out_shape=jax.ShapeDtypeStruct(tensor.shape, BF),
        grid_spec=pltpu.PrefetchScalarGridSpec(
            num_scalar_prefetch=1,
            grid=(rows // step,),
            in_specs=[pl.BlockSpec((step, columns), lambda i, place_ref: (i, 0))],
            out_specs=pl.BlockSpec((step, columns), lambda i, place_ref: (i, 0)),
        ),
        compiler_params=compiler_params(58),
        cost_estimate=pl.CostEstimate(
            flops=4 * rows * columns, bytes_accessed=4 * rows * columns, transcendentals=rows
        ),
        name="normed_blocks",
    )(place, tensor)


def row_switch(run_ref, column, first_row, rows, full_len, seq_count):
    row = first_row + lax.broadcasted_iota(jnp.int32, (rows, 1), 0)
    switch = jnp.zeros((rows, 1), F32)
    for s in range(seq_count):
        inside = (row >= s * full_len) & (row < (s + 1) * full_len)
        switch = jnp.where(inside, run_ref[2 * s + column].astype(F32), switch)
    return switch


def project_kernel(full_len, place_ref, run_ref, tp_ref, heads_ref, *refs):
    weight_refs, hidden_ref, after_ref, normed_ref, total = refs[:4], *refs[4:]
    step = pl.program_id(0)
    rows, _ = hidden_ref.shape
    width = heads_ref.shape[2]

    @pl.when(step == 0)
    def _():
        total[...] = jnp.zeros_like(total)

    first = 0
    for q, weight_ref in enumerate(weight_refs):
        table = 16 + 8 * (q % 2)
        term = None
        for i in range(2):
            source = place_ref[table + 2 * step + i]
            product = dot(heads_ref[source], weight_ref[i * width : (i + 1) * width, :])
            term = product if term is None else term + product
        total[:, first : first + weight_ref.shape[1]] += term
        first += weight_ref.shape[1]

    @pl.when(step == 3)
    def _():
        switch = row_switch(run_ref, 0, tp_ref[0] * rows, rows, full_len, run_ref.shape[0] // 2)
        for j in range(16):
            at = slice(j * LANES, (j + 1) * LANES)
            residual = hidden_ref[:, lanes(place_ref[j])].astype(F32)
            after_ref[:, at] = (residual + switch * total[:, at]).astype(BF)
        widened = after_ref[...].astype(F32)
        normed_ref[...] = (widened * norm_scale(widened)).astype(BF)


def project(place, run_flat, tp_flat, heads, weights, flat_hidden, full_len):
    count, rows, width = heads.shape
    columns = flat_hidden.shape[1]
    depth = count * width
    whole = lambda k, *refs: (0, 0, 0)
    return pl.pallas_call(
        functools.partial(project_kernel, full_len),
        out_shape=[jax.ShapeDtypeStruct((rows, columns), BF)] * 2,
        grid_spec=pltpu.PrefetchScalarGridSpec(
            num_scalar_prefetch=3,
            grid=(4,),
            in_specs=[pl.BlockSpec((count, rows, width), whole)]
            + [pl.BlockSpec((depth // 4, w.shape[1]), lambda k, *refs: (k, 0)) for w in weights]
            + [pl.BlockSpec((rows, columns), lambda k, place, run, tp: (tp[0], 0))],
            out_specs=[pl.BlockSpec((rows, columns), lambda k, *refs: (0, 0))] * 2,
            scratch_shapes=[pltpu.VMEM((rows, columns), F32)],
        ),
        compiler_params=compiler_params(58),
        cost_estimate=pl.CostEstimate(
            flops=2 * rows * depth * columns, bytes_accessed=2 * depth * columns, transcendentals=0
        ),
        name="project",
    )(place, run_flat, tp_flat, heads, *weights, flat_hidden)


def feed_forward_kernel(n_weights, n_in, *refs):
    gates, ups, downs = (refs[i * n_weights : (i + 1) * n_weights] for i in range(3))
    refs = refs[3 * n_weights :]
    in_refs, out_refs = refs[:n_in], refs[n_in:-5]
    rows_ref, gate_ref, up_ref, down_ref, total = refs[-5:]
    step = pl.program_id(0)

    @pl.when(step == 0)
    def _():
        at = 0
        for ref in in_refs:
            rows_ref[at : at + ref.shape[0], :] = ref[...]
            at += ref.shape[0]
        total[...] = jnp.zeros_like(total)

    width = gate_ref.shape[1]
    at = 0
    for gate_piece, up_piece, down_piece in zip(gates, ups, downs):
        depth = gate_piece.shape[0]
        gate_ref[at : at + depth, :] = gate_piece[...]
        up_ref[at : at + depth, :] = up_piece[...]
        for v in range(depth // LANES):
            to = at + v * LANES
            for j in range(width // LANES):
                down_ref[j * LANES : (j + 1) * LANES, to : to + LANES] = down_piece[
                    v * LANES : (v + 1) * LANES, j * LANES : (j + 1) * LANES
                ]
        at += depth
    rows = rows_ref[...]
    gate = dot(rows, gate_ref[...])
    up = dot(rows, up_ref[...])
    hidden = (gate / (1.0 + jnp.exp(-gate)) * up).astype(BF)
    total[...] += dot(hidden, down_ref[...])

    @pl.when(step == pl.num_programs(0) - 1)
    def _():
        at = 0
        for ref in out_refs:
            ref[...] = total[at : at + ref.shape[0], :].astype(BF)
            at += ref.shape[0]


def feed_forward(pieces, outs, weights, ff):
    columns = sum(weight.shape[0] for weight in weights)
    rows = sum(piece.shape[0] for piece in pieces)
    width = 256
    steps = ff // width
    whole = lambda j: (0, 0)

    def specs(first):
        return [pl.BlockSpec((w.shape[0], width), lambda j: (0, j + first)) for w in weights]

    return pl.pallas_call(
        functools.partial(feed_forward_kernel, len(weights), len(pieces)),
        out_shape=[jax.ShapeDtypeStruct((n, columns), BF) for n in outs],
        grid=(steps,),
        in_specs=specs(0)
        + specs(steps)
        + specs(2 * steps)
        + [pl.BlockSpec(piece.shape, whole) for piece in pieces],
        out_specs=[pl.BlockSpec((n, columns), whole) for n in outs],
        scratch_shapes=[
            pltpu.VMEM((rows, columns), BF),
            pltpu.VMEM((columns, width), BF),
            pltpu.VMEM((columns, width), BF),
            pltpu.VMEM((width, columns), BF),
            pltpu.VMEM((rows, columns), F32),
        ],
        compiler_params=compiler_params(58),
        cost_estimate=pl.CostEstimate(
            flops=6 * rows * columns * ff,
            bytes_accessed=6 * columns * ff + 4 * rows * columns,
            transcendentals=rows * ff,
        ),
        name="feed_forward",
    )(*weights, *weights, *weights, *pieces)


def finish_kernel(full_len, first, place_ref, run_ref, tp_ref, after_ref, *refs):
    term_refs, out_ref = refs[:-1], refs[-1]
    rows = out_ref.shape[0]
    own_rows = after_ref.shape[0]
    first_row = tp_ref[0] * own_rows + first
    switch = row_switch(run_ref, 1, first_row, rows, full_len, run_ref.shape[0] // 2)
    for j in range(16):
        at = slice(j * LANES, (j + 1) * LANES)
        total = term_refs[0][:, at].astype(F32)
        for ref in term_refs[1:]:
            total = total + ref[:, at].astype(F32)
        residual = after_ref[first : first + rows, at].astype(F32)
        out_ref[:, lanes(place_ref[j])] = (residual + switch * total).astype(BF)


def finish(place, run_flat, tp_flat, after, first, rows, terms, full_len):
    _, columns = after.shape
    block = lambda i, *refs: (0, 0)
    return pl.pallas_call(
        functools.partial(finish_kernel, full_len, first),
        out_shape=jax.ShapeDtypeStruct((rows, columns), BF),
        grid_spec=pltpu.PrefetchScalarGridSpec(
            num_scalar_prefetch=3,
            grid=(1,),
            in_specs=[pl.BlockSpec(after.shape, block)]
            + [pl.BlockSpec((rows, columns), block)] * len(terms),
            out_specs=pl.BlockSpec((rows, columns), block),
        ),
        compiler_params=compiler_params(58),
        cost_estimate=pl.CostEstimate(
            flops=8 * rows * columns, bytes_accessed=12 * rows * columns, transcendentals=0
        ),
        name="finish",
    )(place, run_flat, tp_flat, after, *terms)


def place_pieces_kernel(items, place_ref, *refs):
    in_refs, out_ref, sems = refs[: len(items)], refs[-2], refs[-1]
    copies = []
    for i, (entry, first) in enumerate(items):
        target = out_ref.at[place_ref[entry], pl.ds(first, in_refs[i].shape[0])]
        copies.append(pltpu.make_async_copy(in_refs[i], target, sems.at[i]))
        copies[-1].start()
    for copy in copies:
        copy.wait()


def place_pieces(place, pieces, items, shape, earlier=None):
    block = lambda i, place_ref: (0, 0)
    held = [] if earlier is None else [earlier]
    return pl.pallas_call(
        functools.partial(place_pieces_kernel, items),
        out_shape=jax.ShapeDtypeStruct(shape, BF),
        grid_spec=pltpu.PrefetchScalarGridSpec(
            num_scalar_prefetch=1,
            grid=(1,),
            in_specs=[pl.BlockSpec(piece.shape, block) for piece in pieces]
            + [pl.BlockSpec(memory_space=pltpu.HBM)] * len(held),
            out_specs=pl.BlockSpec(memory_space=pltpu.HBM),
            scratch_shapes=[pltpu.SemaphoreType.DMA((len(items),))],
        ),
        input_output_aliases={1 + len(pieces): 0} if held else {},
        compiler_params=compiler_params(58),
        cost_estimate=pl.CostEstimate(
            flops=0, bytes_accessed=4 * sum(piece.size for piece in pieces), transcendentals=0
        ),
        name="place_pieces",
    )(place, *pieces, *held)


def places(var_index, tp_index):
    table = PAIR_FIRST + PAIR_FIRST + PAIR_FIRST + RING_FIRST
    back = jnp.array([b for b, _ in table], jnp.int32)
    pair = jnp.array([p for _, p in table], jnp.int32)
    item = jnp.arange(32, dtype=jnp.int32)
    other = (item // 8) % 2
    blocks = ((var_index // 8) ^ pair) * 8 + (((var_index // 2) - back) & 3) * 2
    blocks = blocks + ((var_index % 2) ^ other)
    sources = (((tp_index // 2) - back) & 3) * 2 + ((tp_index % 2) ^ pair)
    return jnp.where(item < 16, blocks, sources).astype(jnp.int32)


def rotary_tables(full_len, width):
    column = jnp.arange(width, dtype=jnp.int32)
    half_width = HEAD_SIZE // 2
    exponent = (column % half_width).astype(F32) * (2.0 / HEAD_SIZE)
    frequency = jnp.power(F32(500000.0), -exponent)
    angles = jnp.arange(full_len, dtype=F32)[:, None] * frequency[None, :]
    turned = (column < width - HEAD_SIZE)[None, :]
    sign = jnp.where(column % HEAD_SIZE < half_width, F32(-1.0), F32(1.0))[None, :]
    cosine = jnp.where(turned, jnp.cos(angles), F32(1.0))
    sine = jnp.where(turned, jnp.sin(angles) * sign, F32(0.0))
    return cosine, sine


def attention_kernel(rows_ref, one_ref, two_ref, cosine_ref, sine_ref, out_ref):
    half = one_ref.shape[0]
    width = one_ref.shape[1]
    projected = dot(rows_ref[:, :half], one_ref[...]) + dot(rows_ref[:, half:], two_ref[...])
    half_width = HEAD_SIZE // 2
    column = lax.broadcasted_iota(jnp.int32, projected.shape, 1)
    swapped = jnp.where(
        (column & half_width) == 0,
        pltpu.roll(projected, width - half_width, 1),
        pltpu.roll(projected, half_width, 1),
    )
    turned = (projected * cosine_ref[...] + swapped * sine_ref[...]).astype(BF)
    queries = width // HEAD_SIZE - 2
    keys = turned[:, queries * HEAD_SIZE : (queries + 1) * HEAD_SIZE]
    values = turned[:, (queries + 1) * HEAD_SIZE :]
    length = rows_ref.shape[0]
    at_query = lax.broadcasted_iota(jnp.int32, (length, length), 0)
    at_key = lax.broadcasted_iota(jnp.int32, (length, length), 1)
    causal = at_query >= at_key
    for h in range(queries):
        query = turned[:, h * HEAD_SIZE : (h + 1) * HEAD_SIZE]
        scores = lax.dot_general(
            query, keys, (((1,), (1,)), ((), ())), preferred_element_type=F32
        ) * (HEAD_SIZE**-0.5)
        scores = jnp.where(causal, scores, F32(-1e30))
        exped = jnp.exp(scores - jnp.max(scores, axis=-1, keepdims=True))
        probs = (exped / jnp.sum(exped, axis=-1, keepdims=True)).astype(BF)
        out_ref[:, h * HEAD_SIZE : (h + 1) * HEAD_SIZE] = dot(probs, values).astype(BF)


def attention(rows, one, two, width, full_len):
    row_count, model_width = rows.shape
    half = one.shape[0]
    out_width = width - 2 * HEAD_SIZE
    cosine, sine = rotary_tables(full_len, width)
    whole = lambda i: (0, 0)
    return pl.pallas_call(
        attention_kernel,
        out_shape=jax.ShapeDtypeStruct((row_count, out_width), BF),
        grid=(row_count // full_len,),
        in_specs=[
            pl.BlockSpec((full_len, model_width), lambda i: (i, 0)),
            pl.BlockSpec((half, width), whole),
            pl.BlockSpec((half, width), whole),
            pl.BlockSpec((full_len, width), whole),
            pl.BlockSpec((full_len, width), whole),
        ],
        out_specs=pl.BlockSpec((full_len, out_width), lambda i: (i, 0)),
        compiler_params=compiler_params(58),
        cost_estimate=pl.CostEstimate(
            flops=2 * row_count * width * model_width + 4 * row_count * full_len * out_width,
            bytes_accessed=2 * row_count * model_width + 4 * half * width,
            transcendentals=row_count * full_len * 4,
        ),
        name="attention",
    )(rows, one, two, cosine, sine)


def layer(hidden_in, run_table, qkv_weight, out_weight, gate_up_weight, down_weight):
    tp_count = lax.axis_size("tp")
    seq_count, full_len, model_width = hidden_in.shape
    row_count = seq_count * full_len
    own_rows = row_count // tp_count
    query_slice = QUERY_HEADS // tp_count
    tp_index = lax.axis_index("tp")
    half = model_width // 2
    place = places(lax.axis_index("var"), tp_index)
    tp_flat = tp_index.astype(jnp.int32).reshape(1)
    run_flat = run_table.reshape(-1)

    def from_partner(tensor):
        return lax.ppermute(tensor, "var", VAR_CORE)

    block = qkv_weight.shape[0]
    width = qkv_weight.shape[1]
    heads_width = query_slice * HEAD_SIZE
    ff_local = gate_up_weight.shape[2]
    out_square = out_weight.reshape(heads_width // block, block, block).transpose(1, 0, 2)
    first_pack = jnp.concatenate([qkv_weight, out_square.reshape(block, heads_width)], axis=1)
    first_pieces = gather_pair_first(first_pack, 0, VAR)
    first_one = jnp.concatenate(first_pieces, axis=0)
    first_two = from_partner(first_one)
    out_block = first_one[:, width:].reshape(half // block, block, heads_width // block, block)
    out_block = out_block.transpose(2, 1, 0, 3).reshape(heads_width, half)
    cut = 640
    ring = gather_ring(out_block[:, cut:], 0, TP)
    ring = jnp.concatenate(ring, axis=0)
    out_b = jnp.concatenate([ring, lax.ppermute(ring, "tp", TP_XL)], axis=0)
    out_a = gather_half(out_block[:, :cut], 0, TP)
    out_weights = [out_a, out_b]
    out_weights = out_weights + [from_partner(w) for w in out_weights]
    down_square = down_weight.reshape(ff_local // block, block, block).transpose(1, 0, 2)
    second_pack = jnp.concatenate(
        [gate_up_weight.reshape(block, 2 * ff_local), down_square.reshape(block, ff_local)], axis=1
    )
    weights = gather_pair_first(second_pack, 0, VAR)
    weights = weights + [from_partner(piece) for piece in weights]

    flat_hidden = hidden_in.reshape(row_count, model_width)
    columns = normed_blocks(place, flat_hidden)
    head_rows = attention(columns, first_one, first_two, width, full_len)
    head_rows = head_rows.reshape(tp_count, own_rows, heads_width)

    heads = lax.all_to_all(head_rows, "tp", split_axis=0, concat_axis=0, tiled=True)
    after_attention, normed_two = project(
        place, run_flat, tp_flat, heads, out_weights, flat_hidden, full_len
    )

    split = 80
    rest = own_rows - split
    in_a = gather_pair_first(normed_two[:split], 0, TP)
    in_b = gather_ring(normed_two[split:], 0, TP)
    cross_b = cross_each(in_b, TP)
    for_own_a, for_own_b, for_back_b, for_ahead_b = feed_forward(
        [in_a[0], in_b[0], in_b[1], in_b[2]], [2 * split, rest, rest, rest], weights, ff_local
    )
    for_back_a, for_ahead_a, for_far_b = feed_forward(
        [in_a[1], in_a[2], in_b[3], in_b[4]], [2 * split, 2 * split, rest], weights, ff_local
    )
    for_far_a, for_cross_b = feed_forward(
        in_a[3:] + cross_b, [2 * split, 4 * rest], weights, ff_local
    )

    terms_a = [
        for_own_a,
        lax.ppermute(for_back_a, "tp", tp_y(3)),
        lax.ppermute(for_ahead_a, "tp", tp_y(1)),
        lax.ppermute(for_far_a, "tp", tp_y(2)),
    ]
    given = sum(term[split:].astype(F32) for term in terms_a).astype(BF)
    terms_a.append(lax.ppermute(given, "tp", TP_XL))
    result_a = finish(
        place, run_flat, tp_flat, after_attention, 0, split, terms_a, full_len
    )
    crossed = lax.ppermute(for_cross_b, "tp", TP_XL)

    def joined(term, k):
        part = crossed[k * rest : (k + 1) * rest]
        return (term.astype(F32) + part.astype(F32)).astype(BF)

    terms_b = [
        for_own_b,
        crossed,
        lax.ppermute(joined(for_back_b, 1), "tp", tp_y(3)),
        lax.ppermute(joined(for_ahead_b, 2), "tp", tp_y(1)),
        lax.ppermute(joined(for_far_b, 3), "tp", tp_y(2)),
    ]
    result_b = finish(
        place, run_flat, tp_flat, after_attention, split, rest, terms_b, full_len
    )

    own, back, ahead, far, far2 = gather_pair_first(result_a, 0, TP)
    ring = gather_ring(result_b, 0, TP)
    cross = cross_each(ring, TP)
    half_rest = rest // 2
    shape = (tp_count, own_rows, model_width)
    pieces = halves(own, 0) + halves(back, 0) + halves(ahead, 0) + ring
    items = [(16 + k, 0) for k in range(6)]
    items += [(24 + k, split) for k in range(4)] + [(27, split + half_rest)]
    gathered = place_pieces(place, pieces, items, shape)
    items = [(22, 0), (23, 0)] + [(28 + k, split) for k in range(4)] + [(31, split + half_rest)]
    gathered = place_pieces(place, [far, far2] + cross, items, shape, gathered)
    return gathered.reshape(seq_count, full_len, model_width)


def solution(mesh):
    return jax.shard_map(
        layer,
        mesh=mesh,
        in_specs=(
            P("var", None, None),
            P("var", None),
            P("var", "tp"),
            P("tp", "var"),
            P("var", None, "tp"),
            P("tp", "var"),
        ),
        out_specs=P("var", None, None),
        check_vma=False,
    )
```

```python
import functools

import jax
import jax.numpy as jnp
from jax import lax
from jax.experimental import pallas as pl
from jax.experimental.pallas import tpu as pltpu
from jax.sharding import PartitionSpec as P


QUERY_HEADS = 32
HEAD_SIZE = 64
BF = jnp.bfloat16
F32 = jnp.float32

VAR_XH = [(v, v ^ 8) for v in range(16)]
VAR_CORE = [(v, v ^ 1) for v in range(16)]
TP_XL = [(t, t ^ 1) for t in range(8)]
PAIR_FIRST = [(0, 0), (0, 1), (1, 0), (1, 1), (3, 0), (3, 1), (2, 0), (2, 1)]
RING_FIRST = [(0, 0), (1, 0), (3, 0), (2, 0), (0, 1), (1, 1), (3, 1), (2, 1)]
LANES = 128


def var_z(step):
    return [(v, (v & 9) | ((((v >> 1) & 3) + step) % 4) << 1) for v in range(16)]


def tp_y(step, pair=0):
    return [(t, (t & 1) ^ pair | (((t >> 1) + step) % 4) << 1) for t in range(8)]


VAR = ("var", VAR_XH, var_z(1), var_z(3))
TP = ("tp", TP_XL, tp_y(1), tp_y(3))


def halves(pair, axis):
    return lax.split(pair, [pair.shape[axis] // 2] * 2, axis=axis)


def gather_pair_first(piece, axis, group):
    name, flip, up, down = group
    own = jnp.concatenate([piece, lax.ppermute(piece, name, flip)], axis=axis)
    back = lax.ppermute(own, name, up)
    ahead = lax.ppermute(own, name, down)
    far = [
        lax.ppermute(halves(back, axis)[0], name, up),
        lax.ppermute(halves(ahead, axis)[1], name, down),
    ]
    return [own, back, ahead] + far


def send_both(piece, group):
    return lax.ppermute(piece, group[0], group[2]), lax.ppermute(piece, group[0], group[3])


def gather_each(piece, group):
    name, flip, up, down = group
    other = lax.ppermute(piece, name, flip)
    back = lax.ppermute(piece, name, up)
    ahead = lax.ppermute(piece, name, down)
    other_back = lax.ppermute(other, name, up)
    other_ahead = lax.ppermute(other, name, down)
    far = lax.ppermute(back, name, up)
    other_far = lax.ppermute(other_ahead, name, down)
    return [piece, other, back, other_back, ahead, other_ahead, far, other_far]


def gather_ring(piece, group):
    name, _, up, down = group
    back = lax.ppermute(piece, name, up)
    ahead = lax.ppermute(piece, name, down)
    return [piece, back, ahead, lax.ppermute(back, name, up)]


def cross_each(pieces, group):
    return [lax.ppermute(piece, group[0], group[1]) for piece in pieces]


def compiler_params(mib):
    return pltpu.CompilerParams(vmem_limit_bytes=mib * 2**20)


def dot(a, b):
    return jnp.dot(a, b, preferred_element_type=F32)


def lanes(block):
    return pl.ds(pl.multiple_of(block * LANES, LANES), LANES)


def norm_scale(widened):
    return lax.rsqrt(jnp.mean(widened * widened, axis=-1, keepdims=True) + 1e-05)


def normed_blocks_kernel(place_ref, in_ref, out_ref):
    @pl.loop(0, in_ref.shape[0] // 64)
    def _(i):
        rows = pl.ds(pl.multiple_of(i * 64, 64), 64)
        scale = norm_scale(in_ref[rows, :].astype(F32))
        for j in range(16):
            block = in_ref[rows, lanes(place_ref[j])].astype(F32)
            out_ref[rows, j * LANES : (j + 1) * LANES] = (block * scale).astype(BF)


def normed_blocks(place, tensor):
    rows, columns = tensor.shape
    step = 384
    return pl.pallas_call(
        normed_blocks_kernel,
        out_shape=jax.ShapeDtypeStruct(tensor.shape, BF),
        grid_spec=pltpu.PrefetchScalarGridSpec(
            num_scalar_prefetch=1,
            grid=(rows // step,),
            in_specs=[pl.BlockSpec((step, columns), lambda i, place_ref: (i, 0))],
            out_specs=pl.BlockSpec((step, columns), lambda i, place_ref: (i, 0)),
        ),
        compiler_params=compiler_params(58),
        cost_estimate=pl.CostEstimate(
            flops=4 * rows * columns, bytes_accessed=4 * rows * columns, transcendentals=rows
        ),
        name="normed_blocks",
    )(place, tensor)


def row_switch(run_ref, column, first_row, rows, full_len, seq_count):
    row = first_row + lax.broadcasted_iota(jnp.int32, (rows, 1), 0)
    switch = jnp.zeros((rows, 1), F32)
    for s in range(seq_count):
        inside = (row >= s * full_len) & (row < (s + 1) * full_len)
        switch = jnp.where(inside, run_ref[2 * s + column].astype(F32), switch)
    return switch


def project_kernel(counts, place_ref, own_ref, other_ref, *refs):
    weight_refs = refs[: sum(counts)]
    own_out, other_out = refs[sum(counts) :]
    rows, width = own_ref.shape[1:]
    first = 0
    for group, count in enumerate(counts):
        entry = 16 + 8 * group
        term = None
        for weight_ref in weight_refs[:count]:
            for i in range(weight_ref.shape[0] // width):
                source = place_ref[entry]
                heads = jnp.concatenate([own_ref[source], other_ref[source]], axis=0)
                product = dot(heads, weight_ref[i * width : (i + 1) * width, :])
                term = product if term is None else term + product
                entry += 1
        at = slice(first, first + term.shape[1])
        own_out[:, at] = term[:rows]
        other_out[:, at] = term[rows:].astype(BF)
        first += term.shape[1]
        weight_refs = weight_refs[count:]


def project(place, own_heads, other_heads, groups):
    count, rows, width = own_heads.shape
    weights = sum(groups, [])
    columns = sum(group[0].shape[1] for group in groups)
    whole = lambda k, *refs: (0, 0)
    heads = pl.BlockSpec((count, rows, width), lambda k, *refs: (0, 0, 0))
    return pl.pallas_call(
        functools.partial(project_kernel, [len(group) for group in groups]),
        out_shape=[jax.ShapeDtypeStruct((rows, columns), kind) for kind in (F32, BF)],
        grid_spec=pltpu.PrefetchScalarGridSpec(
            num_scalar_prefetch=1,
            grid=(1,),
            in_specs=[heads, heads] + [pl.BlockSpec(w.shape, whole) for w in weights],
            out_specs=[pl.BlockSpec((rows, columns), whole)] * 2,
        ),
        compiler_params=compiler_params(58),
        cost_estimate=pl.CostEstimate(
            flops=4 * rows * count * width * columns,
            bytes_accessed=2 * count * width * columns,
            transcendentals=0,
        ),
        name="project",
    )(place, own_heads, other_heads, *weights)


def combine_kernel(full_len, place_ref, run_ref, tp_ref, one_ref, two_ref, hidden_ref, *refs):
    after_ref, normed_a, normed_b, switch_ref = refs
    rows, _ = one_ref.shape
    first_row = tp_ref[0] * rows
    seq_count = run_ref.shape[0] // 2
    switch = row_switch(run_ref, 0, first_row, rows, full_len, seq_count)
    for j in range(16):
        at = slice(j * LANES, (j + 1) * LANES)
        source = one_ref if j < 8 else two_ref
        attention = source[:, j % 8 * LANES : (j % 8 + 1) * LANES].astype(F32)
        residual = hidden_ref[:, lanes(place_ref[j])].astype(F32)
        after_ref[:, at] = (residual + switch * attention).astype(BF)
    switch = row_switch(run_ref, 1, first_row, rows, full_len, seq_count)
    switch_ref[...] = jnp.broadcast_to(switch, switch_ref.shape)
    widened = after_ref[...].astype(F32)
    normed = (widened * norm_scale(widened)).astype(BF)
    split = normed_a.shape[0]
    normed_a[...] = normed[:split]
    normed_b[...] = normed[split:]


def combine(place, run_flat, tp_flat, one, two, flat_hidden, full_len, split):
    rows, half = one.shape
    columns = flat_hidden.shape[1]
    whole = lambda k, *refs: (0, 0)
    counts = (rows, split, rows - split)
    return pl.pallas_call(
        functools.partial(combine_kernel, full_len),
        out_shape=[jax.ShapeDtypeStruct((n, columns), BF) for n in counts]
        + [jax.ShapeDtypeStruct((rows, LANES), F32)],
        grid_spec=pltpu.PrefetchScalarGridSpec(
            num_scalar_prefetch=3,
            grid=(1,),
            in_specs=[pl.BlockSpec((rows, half), whole)] * 2
            + [pl.BlockSpec((rows, columns), lambda k, place, run, tp: (tp[0], 0))],
            out_specs=[pl.BlockSpec((n, columns), whole) for n in counts]
            + [pl.BlockSpec((rows, LANES), whole)],
        ),
        compiler_params=compiler_params(58),
        cost_estimate=pl.CostEstimate(
            flops=8 * rows * columns, bytes_accessed=12 * rows * columns, transcendentals=rows
        ),
        name="combine",
    )(place, run_flat, tp_flat, one, two, flat_hidden)


def collect_rows(in_refs, rows_ref, total):
    at = 0
    for ref in in_refs:
        rows_ref[at : at + ref.shape[0], :] = ref[...]
        at += ref.shape[0]
    total[...] = jnp.zeros_like(total)


def add_block(rows_ref, gate_ref, up_ref, down_ref, total):
    rows = rows_ref[...]
    gate = dot(rows, gate_ref[...])
    up = dot(rows, up_ref[...])
    hidden = (gate / (1.0 + jnp.exp(-gate)) * up).astype(BF)
    total[...] += dot(hidden, down_ref[...])


def store_rows(total, outs, out_refs):
    for ranges, ref in zip(outs, out_refs):
        to = 0
        for first, rows in ranges:
            ref[to : to + rows, :] = total[first : first + rows, :].astype(BF)
            to += rows


def lengths(outs):
    return [sum(rows for _, rows in ranges) for ranges in outs]


def first_feed_forward_kernel(n_weights, n_in, outs, *refs):
    gates, ups, downs = (refs[i * n_weights : (i + 1) * n_weights] for i in range(3))
    refs = refs[3 * n_weights :]
    in_refs, out_refs = refs[:n_in], refs[n_in:-5]
    gate_ref, up_ref, down_ref, rows_ref, total = refs[-5:]
    step = pl.program_id(0)
    pl.when(step == 0)(lambda: collect_rows(in_refs, rows_ref, total))
    width = gate_ref.shape[1]
    at = 0
    for gate_piece, up_piece, down_piece in zip(gates, ups, downs):
        depth = gate_piece.shape[0]
        gate_ref[at : at + depth, :] = gate_piece[...]
        up_ref[at : at + depth, :] = up_piece[...]
        for v in range(depth // LANES):
            to = at + v * LANES
            for j in range(width // LANES):
                down_ref[j * LANES : (j + 1) * LANES, to : to + LANES] = down_piece[
                    v * LANES : (v + 1) * LANES, j * LANES : (j + 1) * LANES
                ]
        at += depth
    add_block(rows_ref, gate_ref, up_ref, down_ref, total)
    pl.when(step == pl.num_programs(0) - 1)(lambda: store_rows(total, outs, out_refs))


def feed_forward_kernel(n_in, outs, gate_ref, up_ref, down_ref, *refs):
    in_refs, out_refs, rows_ref, total = refs[:n_in], refs[n_in:-2], refs[-2], refs[-1]
    step = pl.program_id(0)
    pl.when(step == 0)(lambda: collect_rows(in_refs, rows_ref, total))
    add_block(rows_ref, gate_ref, up_ref, down_ref, total)
    pl.when(step == pl.num_programs(0) - 1)(lambda: store_rows(total, outs, out_refs))


def feed_forward_cost(rows, columns, ff):
    return pl.CostEstimate(
        flops=6 * rows * columns * ff,
        bytes_accessed=6 * columns * ff + 4 * rows * columns,
        transcendentals=rows * ff,
    )


def weight_specs(columns, width):
    return [
        pl.BlockSpec((columns, width), lambda j: (0, j)),
        pl.BlockSpec((columns, width), lambda j: (0, j)),
        pl.BlockSpec((width, columns), lambda j: (j, 0)),
    ]


FF_WIDTH = 256


def first_feed_forward(pieces, outs, weights, ff):
    columns = sum(weight.shape[0] for weight in weights)
    rows = sum(piece.shape[0] for piece in pieces)
    width = FF_WIDTH
    steps = ff // width
    whole = lambda j: (0, 0)

    def specs(first):
        return [pl.BlockSpec((w.shape[0], width), lambda j: (0, j + first)) for w in weights]

    return pl.pallas_call(
        functools.partial(first_feed_forward_kernel, len(weights), len(pieces), outs),
        out_shape=[jax.ShapeDtypeStruct((n, columns), BF) for n in lengths(outs)]
        + [jax.ShapeDtypeStruct(dims, BF) for dims in [(columns, ff)] * 2 + [(ff, columns)]],
        grid=(steps,),
        in_specs=specs(0)
        + specs(steps)
        + specs(2 * steps)
        + [pl.BlockSpec(piece.shape, whole) for piece in pieces],
        out_specs=[pl.BlockSpec((n, columns), whole) for n in lengths(outs)] + weight_specs(columns, width),
        scratch_shapes=[pltpu.VMEM((rows, columns), BF), pltpu.VMEM((rows, columns), F32)],
        compiler_params=compiler_params(58),
        cost_estimate=feed_forward_cost(rows, columns, ff),
        name="first_feed_forward",
    )(*weights, *weights, *weights, *pieces)


def feed_forward(pieces, outs, weights):
    columns, ff = weights[0].shape
    rows = sum(piece.shape[0] for piece in pieces)
    whole = lambda j: (0, 0)
    return pl.pallas_call(
        functools.partial(feed_forward_kernel, len(pieces), outs),
        out_shape=[jax.ShapeDtypeStruct((n, columns), BF) for n in lengths(outs)],
        grid=(ff // FF_WIDTH,),
        in_specs=weight_specs(columns, FF_WIDTH)
        + [pl.BlockSpec(piece.shape, whole) for piece in pieces],
        out_specs=[pl.BlockSpec((n, columns), whole) for n in lengths(outs)],
        scratch_shapes=[pltpu.VMEM((rows, columns), BF), pltpu.VMEM((rows, columns), F32)],
        compiler_params=compiler_params(58),
        cost_estimate=feed_forward_cost(rows, columns, ff),
        name="feed_forward",
    )(*weights, *pieces)


def place_pieces_kernel(items, place_ref, *refs):
    in_refs, (out_ref, held, sems) = refs[: len(items)], refs[-3:]
    copies = []
    at = 0
    for i, (entry, first) in enumerate(items):
        rows = in_refs[i].shape[0]
        for j in range(16):
            block = in_refs[i][:, j * LANES : (j + 1) * LANES]
            held[at : at + rows, lanes(place_ref[j])] = block
        target = out_ref.at[place_ref[entry], pl.ds(first, rows)]
        copies.append(pltpu.make_async_copy(held.at[pl.ds(at, rows)], target, sems.at[i]))
        copies[-1].start()
        at += rows
    for copy in copies:
        copy.wait()


def place_pieces(place, pieces, items, shape, earlier=None):
    block = lambda i, place_ref: (0, 0)
    held = [] if earlier is None else [earlier]
    return pl.pallas_call(
        functools.partial(place_pieces_kernel, items),
        out_shape=jax.ShapeDtypeStruct(shape, BF),
        grid_spec=pltpu.PrefetchScalarGridSpec(
            num_scalar_prefetch=1,
            grid=(1,),
            in_specs=[pl.BlockSpec(piece.shape, block) for piece in pieces]
            + [pl.BlockSpec(memory_space=pltpu.HBM)] * len(held),
            out_specs=pl.BlockSpec(memory_space=pltpu.HBM),
            scratch_shapes=[
                pltpu.VMEM((sum(piece.shape[0] for piece in pieces), shape[2]), BF),
                pltpu.SemaphoreType.DMA((len(items),)),
            ],
        ),
        input_output_aliases={1 + len(pieces): 0} if held else {},
        compiler_params=compiler_params(58),
        cost_estimate=pl.CostEstimate(
            flops=0, bytes_accessed=4 * sum(piece.size for piece in pieces), transcendentals=0
        ),
        name="place_pieces",
    )(place, *pieces, *held)


def places(var_index, tp_index):
    table = PAIR_FIRST + PAIR_FIRST + PAIR_FIRST + RING_FIRST
    back = jnp.array([b for b, _ in table], jnp.int32)
    pair = jnp.array([p for _, p in table], jnp.int32)
    item = jnp.arange(32, dtype=jnp.int32)
    other = (item // 8) % 2
    blocks = ((var_index // 8) ^ pair) * 8 + (((var_index // 2) - back) & 3) * 2
    blocks = blocks + ((var_index % 2) ^ other)
    sources = (((tp_index // 2) - back) & 3) * 2 + ((tp_index % 2) ^ pair)
    return jnp.where(item < 16, blocks, sources).astype(jnp.int32)


def rotary_tables(full_len):
    column = jnp.arange(LANES, dtype=jnp.int32)
    half_width = HEAD_SIZE // 2
    exponent = (column % half_width).astype(F32) * (2.0 / HEAD_SIZE)
    frequency = jnp.power(F32(500000.0), -exponent)
    angles = jnp.arange(full_len, dtype=F32)[:, None] * frequency[None, :]
    sign = jnp.where(column % HEAD_SIZE < half_width, F32(-1.0), F32(1.0))[None, :]
    return jnp.cos(angles), jnp.sin(angles) * sign


def attention_kernel(rows_ref, one_ref, two_ref, cosine_ref, sine_ref, out_ref):
    half, width = one_ref.shape
    length = rows_ref.shape[0]
    projected = dot(rows_ref[:, :half], one_ref[...]) + dot(rows_ref[:, half:], two_ref[...])
    half_width = HEAD_SIZE // 2
    column = lax.broadcasted_iota(jnp.int32, (length, LANES), 1)
    lower = (column & half_width) == 0
    tiles = []
    for first in range(0, width, LANES):
        tile = projected[:, first : first + LANES]
        swapped = jnp.where(
            lower,
            pltpu.roll(tile, LANES - half_width, 1),
            pltpu.roll(tile, half_width, 1),
        )
        turned = tile * cosine_ref[...] + swapped * sine_ref[...]
        if first + LANES == width:
            turned = jnp.where(column < HEAD_SIZE, turned, tile)
        tiles.append(turned.astype(BF))
    keys = tiles[-1][:, :HEAD_SIZE]
    values = tiles[-1][:, HEAD_SIZE:]
    causal = lax.broadcasted_iota(jnp.int32, (length, length), 0) >= lax.broadcasted_iota(
        jnp.int32, (length, length), 1
    )
    for h in range(width // HEAD_SIZE - 2):
        lane = h * HEAD_SIZE % LANES
        query = tiles[h * HEAD_SIZE // LANES][:, lane : lane + HEAD_SIZE]
        scores = lax.dot_general(
            query, keys, (((1,), (1,)), ((), ())), preferred_element_type=F32
        ) * (HEAD_SIZE**-0.5)
        scores = jnp.where(causal, scores, F32(-1e30))
        exped = jnp.exp(scores - jnp.max(scores, axis=-1, keepdims=True))
        probs = (exped / jnp.sum(exped, axis=-1, keepdims=True)).astype(BF)
        out_ref[:, h * HEAD_SIZE : (h + 1) * HEAD_SIZE] = dot(probs, values).astype(BF)


def attention(rows, one, two, width, cosine, sine):
    row_count, model_width = rows.shape
    half = one.shape[0]
    full_len = cosine.shape[0]
    out_width = width - 2 * HEAD_SIZE
    whole = lambda i: (0, 0)
    return pl.pallas_call(
        attention_kernel,
        out_shape=jax.ShapeDtypeStruct((row_count, out_width), BF),
        grid=(row_count // full_len,),
        in_specs=[
            pl.BlockSpec((full_len, model_width), lambda i: (i, 0)),
            pl.BlockSpec((half, width), whole),
            pl.BlockSpec((half, width), whole),
            pl.BlockSpec(cosine.shape, whole),
            pl.BlockSpec(sine.shape, whole),
        ],
        out_specs=pl.BlockSpec((full_len, out_width), lambda i: (i, 0)),
        compiler_params=compiler_params(58),
        cost_estimate=pl.CostEstimate(
            flops=2 * row_count * width * model_width + 4 * row_count * full_len * out_width,
            bytes_accessed=2 * row_count * model_width + 4 * half * width,
            transcendentals=row_count * full_len * 4,
        ),
        name="attention",
    )(rows, one, two, cosine, sine)


def after(value, *earlier):
    return lax.optimization_barrier((value,) + earlier)[0]


def layer(hidden_in, run_table, qkv_weight, out_weight, gate_up_weight, down_weight):
    tp_count = lax.axis_size("tp")
    seq_count, full_len, model_width = hidden_in.shape
    row_count = seq_count * full_len
    own_rows = row_count // tp_count
    query_slice = QUERY_HEADS // tp_count
    tp_index = lax.axis_index("tp")
    half = model_width // 2
    place = places(lax.axis_index("var"), tp_index)
    tp_flat = tp_index.astype(jnp.int32).reshape(1)
    run_flat = run_table.reshape(-1)

    def from_partner(tensor):
        return lax.ppermute(tensor, "var", VAR_CORE)

    block = qkv_weight.shape[0]
    width = qkv_weight.shape[1]
    heads_width = query_slice * HEAD_SIZE
    ff_local = gate_up_weight.shape[2]
    out_square = out_weight.reshape(heads_width // block, block, block).transpose(1, 0, 2)
    first_pack = jnp.concatenate([qkv_weight, out_square.reshape(block, heads_width)], axis=1)
    first_pieces = gather_pair_first(first_pack, 0, VAR)
    first_one = jnp.concatenate(first_pieces, axis=0)
    first_two = from_partner(first_one)
    out_block = first_one[:, width:].reshape(half // block, block, heads_width // block, block)
    out_block = out_block.transpose(2, 1, 0, 3).reshape(heads_width, half)
    out_pieces = gather_pair_first(out_block, 0, TP)
    down_square = down_weight.reshape(ff_local // block, block, block).transpose(1, 0, 2)
    second_pack = jnp.concatenate(
        [gate_up_weight.reshape(block, 2 * ff_local), down_square.reshape(block, ff_local)], axis=1
    )
    weights = gather_pair_first(second_pack, 0, VAR)
    weights = weights + [from_partner(piece) for piece in weights]

    flat_hidden = hidden_in.reshape(row_count, model_width)
    cosine, sine = rotary_tables(full_len)
    columns = normed_blocks(after(place, cosine, sine), flat_hidden)
    head_rows = attention(columns, first_one, first_two, width, cosine, sine)
    head_rows = head_rows.reshape(tp_count, own_rows, heads_width)

    split = 80
    rest = own_rows - split
    heads = lax.all_to_all(head_rows, "tp", split_axis=0, concat_axis=0, tiled=True)
    other_heads = from_partner(heads)
    one, for_partner = project(place, heads, other_heads, [out_pieces])
    two = from_partner(for_partner)
    after_attention, normed_a, normed_b, switch = combine(
        place, run_flat, tp_flat, one, two, flat_hidden, full_len, split
    )

    other_a = lax.ppermute(normed_a, "tp", TP_XL)
    back_b, ahead_b = send_both(normed_b, TP)
    back_a, ahead_a = send_both(normed_a, TP)
    other_back_a, other_ahead_a = send_both(other_a, TP)
    pair = 2 * split
    for_own, for_pair_a, *joined = first_feed_forward(
        [normed_a, other_a, normed_b],
        [[(0, split), (pair, rest)], [(split, split)]],
        weights,
        ff_local,
    )
    far_a = lax.ppermute(after(back_a, for_pair_a), "tp", TP[2])
    other_far_a = lax.ppermute(after(other_ahead_a, for_pair_a), "tp", TP[3])
    far_b = lax.ppermute(after(back_b, for_pair_a), "tp", TP[2])
    in_a = [normed_a, other_a, back_a, other_back_a, ahead_a, other_ahead_a, far_a, other_far_a]
    in_b = [normed_b, back_b, ahead_b, far_b]
    cross_b = cross_each([normed_b] + [after(t, for_pair_a) for t in in_b[1:]], TP)
    for_back, for_ahead, for_back_pair_a, for_ahead_pair_a = feed_forward(
        in_a[2:6] + in_b[1:3],
        [
            [(0, split), (2 * pair, rest)],
            [(pair, split), (2 * pair + rest, rest)],
            [(split, split)],
            [(pair + split, split)],
        ],
        joined,
    )
    for_far, for_far_pair, for_back_pair_b, for_ahead_pair_b, for_pair_b = feed_forward(
        [in_a[6], in_b[3], in_a[7], cross_b[3], cross_b[1], cross_b[2], cross_b[0]],
        [[(0, own_rows)], [(own_rows, own_rows)]]
        + [[(2 * own_rows + k * rest, rest)] for k in range(3)],
        joined,
    )

    for_far_pair = lax.ppermute(for_far_pair, "tp", TP_XL)
    for_far = (for_far.astype(F32) + for_far_pair.astype(F32)).astype(BF)
    whole_terms = [
        for_own,
        lax.ppermute(for_back, "tp", tp_y(3)),
        lax.ppermute(for_ahead, "tp", tp_y(1)),
        lax.ppermute(for_far, "tp", tp_y(2)),
    ]
    terms_a = [term[:split] for term in whole_terms] + [
        lax.ppermute(for_pair_a, "tp", TP_XL),
        lax.ppermute(for_back_pair_a, "tp", tp_y(3, 1)),
        lax.ppermute(for_ahead_pair_a, "tp", tp_y(1, 1)),
    ]
    terms_b = [term[split:] for term in whole_terms] + [
        lax.ppermute(for_back_pair_b, "tp", tp_y(3, 1)),
        lax.ppermute(for_ahead_pair_b, "tp", tp_y(1, 1)),
        lax.ppermute(for_pair_b, "tp", TP_XL),
    ]

    def finished(rows, terms):
        mlp = sum(term.astype(F32) for term in terms)
        return (after_attention[rows].astype(F32) + switch[rows, :1] * mlp).astype(BF)

    result_a = finished(slice(0, split), terms_a)
    result_b = finished(slice(split, own_rows), terms_b)

    parts_a = gather_each(result_a, TP)
    parts_b = gather_ring(result_b, TP)
    cross = cross_each(parts_b, TP)
    shape = (tp_count, own_rows, model_width)
    pieces = parts_a[:6] + parts_b
    items = [(16 + k, 0) for k in range(6)]
    items += [(24 + k, split) for k in range(4)]
    gathered = place_pieces(place, pieces, items, shape)
    items = [(22, 0), (23, 0)] + [(28 + k, split) for k in range(4)]
    gathered = place_pieces(place, parts_a[6:] + cross, items, shape, gathered)
    return gathered.reshape(seq_count, full_len, model_width)


def solution(mesh):
    return jax.shard_map(
        layer,
        mesh=mesh,
        in_specs=(
            P("var", None, None),
            P("var", None),
            P("var", "tp"),
            P("tp", "var"),
            P("var", None, "tp"),
            P("tp", "var"),
        ),
        out_specs=P("var", None, None),
        check_vma=False,
    )
```

```python
import functools

import jax
import jax.numpy as jnp
from jax import lax
from jax.experimental import pallas as pl
from jax.experimental.pallas import tpu as pltpu
from jax.sharding import PartitionSpec as P


QUERY_HEADS = 32
HEAD_SIZE = 64
BF = jnp.bfloat16
F32 = jnp.float32

VAR_XH = [(v, v ^ 8) for v in range(16)]
VAR_CORE = [(v, v ^ 1) for v in range(16)]
TP_XL = [(t, t ^ 1) for t in range(8)]
PAIR_FIRST = [(0, 0), (0, 1), (1, 0), (1, 1), (3, 0), (3, 1), (2, 0), (2, 1)]
RING_FIRST = [(0, 0), (1, 0), (3, 0), (2, 0), (0, 1), (1, 1), (3, 1), (2, 1)]
LANES = 128


def var_z(step):
    return [(v, (v & 9) | ((((v >> 1) & 3) + step) % 4) << 1) for v in range(16)]


def tp_y(step, pair=0):
    return [(t, (t & 1) ^ pair | (((t >> 1) + step) % 4) << 1) for t in range(8)]


VAR = ("var", VAR_XH, var_z(1), var_z(3))
TP = ("tp", TP_XL, tp_y(1), tp_y(3))


def halves(pair, axis):
    return lax.split(pair, [pair.shape[axis] // 2] * 2, axis=axis)


def gather_pair_first(piece, axis, group):
    name, flip, up, down = group
    own = jnp.concatenate([piece, lax.ppermute(piece, name, flip)], axis=axis)
    back = lax.ppermute(own, name, up)
    ahead = lax.ppermute(own, name, down)
    far = [
        lax.ppermute(halves(back, axis)[0], name, up),
        lax.ppermute(halves(ahead, axis)[1], name, down),
    ]
    return [own, back, ahead] + far


def send_both(piece, group):
    return lax.ppermute(piece, group[0], group[2]), lax.ppermute(piece, group[0], group[3])


def gather_each(piece, group):
    name, flip, up, down = group
    other = lax.ppermute(piece, name, flip)
    back = lax.ppermute(piece, name, up)
    ahead = lax.ppermute(piece, name, down)
    other_back = lax.ppermute(other, name, up)
    other_ahead = lax.ppermute(other, name, down)
    far = lax.ppermute(back, name, up)
    other_far = lax.ppermute(other_ahead, name, down)
    return [piece, other, back, other_back, ahead, other_ahead, far, other_far]


def gather_ring(piece, group):
    name, _, up, down = group
    back = lax.ppermute(piece, name, up)
    ahead = lax.ppermute(piece, name, down)
    return [piece, back, ahead, lax.ppermute(back, name, up)]


def cross_each(pieces, group):
    return [lax.ppermute(piece, group[0], group[1]) for piece in pieces]


def compiler_params(mib):
    return pltpu.CompilerParams(vmem_limit_bytes=mib * 2**20)


def dot(a, b):
    return jnp.dot(a, b, preferred_element_type=F32)


def lanes(block):
    return pl.ds(pl.multiple_of(block * LANES, LANES), LANES)


def norm_scale(widened):
    return lax.rsqrt(jnp.mean(widened * widened, axis=-1, keepdims=True) + 1e-05)


def normed_blocks_kernel(place_ref, in_ref, out_ref):
    @pl.loop(0, in_ref.shape[0] // 64)
    def _(i):
        rows = pl.ds(pl.multiple_of(i * 64, 64), 64)
        scale = norm_scale(in_ref[rows, :].astype(F32))
        for j in range(16):
            block = in_ref[rows, lanes(place_ref[j])].astype(F32)
            out_ref[rows, j * LANES : (j + 1) * LANES] = (block * scale).astype(BF)


def normed_blocks(place, tensor):
    rows, columns = tensor.shape
    step = 384
    return pl.pallas_call(
        normed_blocks_kernel,
        out_shape=jax.ShapeDtypeStruct(tensor.shape, BF),
        grid_spec=pltpu.PrefetchScalarGridSpec(
            num_scalar_prefetch=1,
            grid=(rows // step,),
            in_specs=[pl.BlockSpec((step, columns), lambda i, place_ref: (i, 0))],
            out_specs=pl.BlockSpec((step, columns), lambda i, place_ref: (i, 0)),
        ),
        compiler_params=compiler_params(58),
        cost_estimate=pl.CostEstimate(
            flops=4 * rows * columns, bytes_accessed=4 * rows * columns, transcendentals=rows
        ),
        name="normed_blocks",
    )(place, tensor)


def row_switch(run_ref, column, first_row, rows, full_len, seq_count):
    row = first_row + lax.broadcasted_iota(jnp.int32, (rows, 1), 0)
    switch = jnp.zeros((rows, 1), F32)
    for s in range(seq_count):
        inside = (row >= s * full_len) & (row < (s + 1) * full_len)
        switch = jnp.where(inside, run_ref[2 * s + column].astype(F32), switch)
    return switch


def project_kernel(counts, place_ref, own_ref, other_ref, *refs):
    weight_refs = refs[: sum(counts)]
    own_out, other_out = refs[sum(counts) :]
    rows, width = own_ref.shape[1:]
    first = 0
    for group, count in enumerate(counts):
        entry = 24 + 8 * group
        term = None
        for weight_ref in weight_refs[:count]:
            for i in range(weight_ref.shape[0] // width):
                source = place_ref[entry]
                heads = jnp.concatenate([own_ref[source], other_ref[source]], axis=0)
                product = dot(heads, weight_ref[i * width : (i + 1) * width, :])
                term = product if term is None else term + product
                entry += 1
        at = slice(first, first + term.shape[1])
        own_out[:, at] = term[:rows]
        other_out[:, at] = term[rows:].astype(BF)
        first += term.shape[1]
        weight_refs = weight_refs[count:]


def project(place, own_heads, other_heads, groups):
    count, rows, width = own_heads.shape
    weights = sum(groups, [])
    columns = sum(group[0].shape[1] for group in groups)
    whole = lambda k, *refs: (0, 0)
    heads = pl.BlockSpec((count, rows, width), lambda k, *refs: (0, 0, 0))
    return pl.pallas_call(
        functools.partial(project_kernel, [len(group) for group in groups]),
        out_shape=[jax.ShapeDtypeStruct((rows, columns), kind) for kind in (F32, BF)],
        grid_spec=pltpu.PrefetchScalarGridSpec(
            num_scalar_prefetch=1,
            grid=(1,),
            in_specs=[heads, heads] + [pl.BlockSpec(w.shape, whole) for w in weights],
            out_specs=[pl.BlockSpec((rows, columns), whole)] * 2,
        ),
        compiler_params=compiler_params(58),
        cost_estimate=pl.CostEstimate(
            flops=4 * rows * count * width * columns,
            bytes_accessed=2 * count * width * columns,
            transcendentals=0,
        ),
        name="project",
    )(place, own_heads, other_heads, *weights)


def combine_kernel(full_len, place_ref, run_ref, tp_ref, one_ref, two_ref, hidden_ref, *refs):
    after_ref, normed_a, normed_b, switch_ref = refs
    rows, _ = one_ref.shape
    first_row = tp_ref[0] * rows
    seq_count = run_ref.shape[0] // 2
    switch = row_switch(run_ref, 0, first_row, rows, full_len, seq_count)
    for j in range(16):
        at = slice(j * LANES, (j + 1) * LANES)
        source = one_ref if j < 8 else two_ref
        attention = source[:, j % 8 * LANES : (j % 8 + 1) * LANES].astype(F32)
        residual = hidden_ref[:, lanes(place_ref[j])].astype(F32)
        after_ref[:, at] = (residual + switch * attention).astype(BF)
    switch = row_switch(run_ref, 1, first_row, rows, full_len, seq_count)
    switch_ref[...] = jnp.broadcast_to(switch, switch_ref.shape)
    widened = after_ref[...].astype(F32)
    normed = (widened * norm_scale(widened)).astype(BF)
    split = normed_a.shape[0]
    normed_a[...] = normed[:split]
    normed_b[...] = normed[split:]


def combine(place, run_flat, tp_flat, one, two, flat_hidden, full_len, split):
    rows, half = one.shape
    columns = flat_hidden.shape[1]
    whole = lambda k, *refs: (0, 0)
    counts = (rows, split, rows - split)
    return pl.pallas_call(
        functools.partial(combine_kernel, full_len),
        out_shape=[jax.ShapeDtypeStruct((n, columns), BF) for n in counts]
        + [jax.ShapeDtypeStruct((rows, LANES), F32)],
        grid_spec=pltpu.PrefetchScalarGridSpec(
            num_scalar_prefetch=3,
            grid=(1,),
            in_specs=[pl.BlockSpec((rows, half), whole)] * 2
            + [pl.BlockSpec((rows, columns), lambda k, place, run, tp: (tp[0], 0))],
            out_specs=[pl.BlockSpec((n, columns), whole) for n in counts]
            + [pl.BlockSpec((rows, LANES), whole)],
        ),
        compiler_params=compiler_params(58),
        cost_estimate=pl.CostEstimate(
            flops=8 * rows * columns, bytes_accessed=12 * rows * columns, transcendentals=rows
        ),
        name="combine",
    )(place, run_flat, tp_flat, one, two, flat_hidden)


def collect_rows(in_refs, rows_ref, total):
    at = 0
    for ref in in_refs:
        rows_ref[at : at + ref.shape[0], :] = ref[...]
        at += ref.shape[0]
    total[...] = jnp.zeros_like(total)


def add_block(rows_ref, gate_ref, up_ref, down_ref, total):
    rows = rows_ref[...]
    gate = dot(rows, gate_ref[...])
    up = dot(rows, up_ref[...])
    hidden = (gate / (1.0 + jnp.exp(-gate)) * up).astype(BF)
    total[...] += dot(hidden, down_ref[...])


def store_rows(total, outs, out_refs):
    for ranges, ref in zip(outs, out_refs):
        to = 0
        for first, rows in ranges:
            ref[to : to + rows, :] = total[first : first + rows, :].astype(BF)
            to += rows


def lengths(outs):
    return [sum(rows for _, rows in ranges) for ranges in outs]


def first_feed_forward_kernel(n_weights, n_in, outs, *refs):
    gates, ups, downs = (refs[i * n_weights : (i + 1) * n_weights] for i in range(3))
    refs = refs[3 * n_weights :]
    in_refs, out_refs = refs[:n_in], refs[n_in:-5]
    gate_ref, up_ref, down_ref, rows_ref, total = refs[-5:]
    step = pl.program_id(0)
    pl.when(step == 0)(lambda: collect_rows(in_refs, rows_ref, total))
    width = gate_ref.shape[1]
    at = 0
    for gate_piece, up_piece, down_piece in zip(gates, ups, downs):
        depth = gate_piece.shape[0]
        gate_ref[at : at + depth, :] = gate_piece[...]
        up_ref[at : at + depth, :] = up_piece[...]
        for v in range(depth // LANES):
            to = at + v * LANES
            for j in range(width // LANES):
                down_ref[j * LANES : (j + 1) * LANES, to : to + LANES] = down_piece[
                    v * LANES : (v + 1) * LANES, j * LANES : (j + 1) * LANES
                ]
        at += depth
    add_block(rows_ref, gate_ref, up_ref, down_ref, total)
    pl.when(step == pl.num_programs(0) - 1)(lambda: store_rows(total, outs, out_refs))


def feed_forward_kernel(n_in, outs, gate_ref, up_ref, down_ref, *refs):
    in_refs, out_refs, rows_ref, total = refs[:n_in], refs[n_in:-2], refs[-2], refs[-1]
    step = pl.program_id(0)
    pl.when(step == 0)(lambda: collect_rows(in_refs, rows_ref, total))
    add_block(rows_ref, gate_ref, up_ref, down_ref, total)
    pl.when(step == pl.num_programs(0) - 1)(lambda: store_rows(total, outs, out_refs))


def feed_forward_cost(rows, columns, ff):
    return pl.CostEstimate(
        flops=6 * rows * columns * ff,
        bytes_accessed=6 * columns * ff + 4 * rows * columns,
        transcendentals=rows * ff,
    )


def weight_specs(columns, width):
    return [
        pl.BlockSpec((columns, width), lambda j: (0, j)),
        pl.BlockSpec((columns, width), lambda j: (0, j)),
        pl.BlockSpec((width, columns), lambda j: (j, 0)),
    ]


FF_WIDTH = 256


def first_feed_forward(pieces, outs, weights, ff):
    columns = sum(weight.shape[0] for weight in weights)
    rows = sum(piece.shape[0] for piece in pieces)
    width = FF_WIDTH
    steps = ff // width
    whole = lambda j: (0, 0)

    def specs(first):
        return [pl.BlockSpec((w.shape[0], width), lambda j: (0, j + first)) for w in weights]

    return pl.pallas_call(
        functools.partial(first_feed_forward_kernel, len(weights), len(pieces), outs),
        out_shape=[jax.ShapeDtypeStruct((n, columns), BF) for n in lengths(outs)]
        + [jax.ShapeDtypeStruct(dims, BF) for dims in [(columns, ff)] * 2 + [(ff, columns)]],
        grid=(steps,),
        in_specs=specs(0)
        + specs(steps)
        + specs(2 * steps)
        + [pl.BlockSpec(piece.shape, whole) for piece in pieces],
        out_specs=[pl.BlockSpec((n, columns), whole) for n in lengths(outs)] + weight_specs(columns, width),
        scratch_shapes=[pltpu.VMEM((rows, columns), BF), pltpu.VMEM((rows, columns), F32)],
        compiler_params=compiler_params(58),
        cost_estimate=feed_forward_cost(rows, columns, ff),
        name="first_feed_forward",
    )(*weights, *weights, *weights, *pieces)


def feed_forward(pieces, outs, weights):
    columns, ff = weights[0].shape
    rows = sum(piece.shape[0] for piece in pieces)
    whole = lambda j: (0, 0)
    return pl.pallas_call(
        functools.partial(feed_forward_kernel, len(pieces), outs),
        out_shape=[jax.ShapeDtypeStruct((n, columns), BF) for n in lengths(outs)],
        grid=(ff // FF_WIDTH,),
        in_specs=weight_specs(columns, FF_WIDTH)
        + [pl.BlockSpec(piece.shape, whole) for piece in pieces],
        out_specs=[pl.BlockSpec((n, columns), whole) for n in lengths(outs)],
        scratch_shapes=[pltpu.VMEM((rows, columns), BF), pltpu.VMEM((rows, columns), F32)],
        compiler_params=compiler_params(58),
        cost_estimate=feed_forward_cost(rows, columns, ff),
        name="feed_forward",
    )(*weights, *pieces)


def place_pieces_kernel(items, place_ref, *refs):
    in_refs, (out_ref, held, sems) = refs[: len(items)], refs[-3:]
    copies = []
    at = 0
    for i, (entry, first) in enumerate(items):
        rows = in_refs[i].shape[0]
        for j in range(16):
            block = in_refs[i][:, j * LANES : (j + 1) * LANES]
            held[at : at + rows, lanes(place_ref[j])] = block
        target = out_ref.at[place_ref[entry], pl.ds(first, rows)]
        copies.append(pltpu.make_async_copy(held.at[pl.ds(at, rows)], target, sems.at[i]))
        copies[-1].start()
        at += rows
    for copy in copies:
        copy.wait()


def place_pieces(place, pieces, items, shape, earlier=None):
    block = lambda i, place_ref: (0, 0)
    held = [] if earlier is None else [earlier]
    return pl.pallas_call(
        functools.partial(place_pieces_kernel, items),
        out_shape=jax.ShapeDtypeStruct(shape, BF),
        grid_spec=pltpu.PrefetchScalarGridSpec(
            num_scalar_prefetch=1,
            grid=(1,),
            in_specs=[pl.BlockSpec(piece.shape, block) for piece in pieces]
            + [pl.BlockSpec(memory_space=pltpu.HBM)] * len(held),
            out_specs=pl.BlockSpec(memory_space=pltpu.HBM),
            scratch_shapes=[
                pltpu.VMEM((sum(piece.shape[0] for piece in pieces), shape[2]), BF),
                pltpu.SemaphoreType.DMA((len(items),)),
            ],
        ),
        input_output_aliases={1 + len(pieces): 0} if held else {},
        compiler_params=compiler_params(58),
        cost_estimate=pl.CostEstimate(
            flops=0, bytes_accessed=4 * sum(piece.size for piece in pieces), transcendentals=0
        ),
        name="place_pieces",
    )(place, *pieces, *held)


def places(var_index, tp_index):
    table = PAIR_FIRST + PAIR_FIRST + PAIR_FIRST + RING_FIRST
    back = jnp.array([b for b, _ in table], jnp.int32)
    pair = jnp.array([p for _, p in table], jnp.int32)
    item = jnp.arange(32, dtype=jnp.int32)
    other = (item // 8) % 2
    blocks = ((var_index // 8) ^ pair) * 8 + (((var_index // 2) - back) & 3) * 2
    blocks = blocks + ((var_index % 2) ^ other)
    sources = (((tp_index // 2) - back) & 3) * 2 + ((tp_index % 2) ^ pair)
    return jnp.where(item < 16, blocks, sources).astype(jnp.int32)


def rotary_tables(full_len):
    column = jnp.arange(LANES, dtype=jnp.int32)
    half_width = HEAD_SIZE // 2
    exponent = (column % half_width).astype(F32) * (2.0 / HEAD_SIZE)
    frequency = jnp.power(F32(500000.0), -exponent)
    angles = jnp.arange(full_len, dtype=F32)[:, None] * frequency[None, :]
    sign = jnp.where(column % HEAD_SIZE < half_width, F32(-1.0), F32(1.0))[None, :]
    return jnp.cos(angles), jnp.sin(angles) * sign


def attention_kernel(rows_ref, one_ref, two_ref, cosine_ref, sine_ref, out_ref):
    half, width = one_ref.shape
    length = rows_ref.shape[0]
    projected = dot(rows_ref[:, :half], one_ref[...]) + dot(rows_ref[:, half:], two_ref[...])
    half_width = HEAD_SIZE // 2
    column = lax.broadcasted_iota(jnp.int32, (length, LANES), 1)
    lower = (column & half_width) == 0
    tiles = []
    for first in range(0, width, LANES):
        tile = projected[:, first : first + LANES]
        swapped = jnp.where(
            lower,
            pltpu.roll(tile, LANES - half_width, 1),
            pltpu.roll(tile, half_width, 1),
        )
        turned = tile * cosine_ref[...] + swapped * sine_ref[...]
        if first + LANES == width:
            turned = jnp.where(column < HEAD_SIZE, turned, tile)
        tiles.append(turned.astype(BF))
    keys = tiles[-1][:, :HEAD_SIZE]
    values = tiles[-1][:, HEAD_SIZE:]
    causal = lax.broadcasted_iota(jnp.int32, (length, length), 0) >= lax.broadcasted_iota(
        jnp.int32, (length, length), 1
    )
    for h in range(width // HEAD_SIZE - 2):
        lane = h * HEAD_SIZE % LANES
        query = tiles[h * HEAD_SIZE // LANES][:, lane : lane + HEAD_SIZE]
        scores = lax.dot_general(
            query, keys, (((1,), (1,)), ((), ())), preferred_element_type=F32
        ) * (HEAD_SIZE**-0.5)
        scores = jnp.where(causal, scores, F32(-1e30))
        exped = jnp.exp(scores - jnp.max(scores, axis=-1, keepdims=True))
        probs = (exped / jnp.sum(exped, axis=-1, keepdims=True)).astype(BF)
        out_ref[:, h * HEAD_SIZE : (h + 1) * HEAD_SIZE] = dot(probs, values).astype(BF)


def attention(rows, one, two, width, cosine, sine):
    row_count, model_width = rows.shape
    half = one.shape[0]
    full_len = cosine.shape[0]
    out_width = width - 2 * HEAD_SIZE
    whole = lambda i: (0, 0)
    return pl.pallas_call(
        attention_kernel,
        out_shape=jax.ShapeDtypeStruct((row_count, out_width), BF),
        grid=(row_count // full_len,),
        in_specs=[
            pl.BlockSpec((full_len, model_width), lambda i: (i, 0)),
            pl.BlockSpec((half, width), whole),
            pl.BlockSpec((half, width), whole),
            pl.BlockSpec(cosine.shape, whole),
            pl.BlockSpec(sine.shape, whole),
        ],
        out_specs=pl.BlockSpec((full_len, out_width), lambda i: (i, 0)),
        compiler_params=compiler_params(58),
        cost_estimate=pl.CostEstimate(
            flops=2 * row_count * width * model_width + 4 * row_count * full_len * out_width,
            bytes_accessed=2 * row_count * model_width + 4 * half * width,
            transcendentals=row_count * full_len * 4,
        ),
        name="attention",
    )(rows, one, two, cosine, sine)


def after(value, *earlier):
    return lax.optimization_barrier((value,) + earlier)[0]


def layer(hidden_in, run_table, qkv_weight, out_weight, gate_up_weight, down_weight):
    tp_count = lax.axis_size("tp")
    seq_count, full_len, model_width = hidden_in.shape
    row_count = seq_count * full_len
    own_rows = row_count // tp_count
    query_slice = QUERY_HEADS // tp_count
    tp_index = lax.axis_index("tp")
    half = model_width // 2
    place = places(lax.axis_index("var"), tp_index)
    tp_flat = tp_index.astype(jnp.int32).reshape(1)
    run_flat = run_table.reshape(-1)

    def from_partner(tensor):
        return lax.ppermute(tensor, "var", VAR_CORE)

    block = qkv_weight.shape[0]
    width = qkv_weight.shape[1]
    heads_width = query_slice * HEAD_SIZE
    ff_local = gate_up_weight.shape[2]
    out_square = out_weight.reshape(heads_width // block, block, block).transpose(1, 0, 2)
    first_pack = jnp.concatenate([qkv_weight, out_square.reshape(block, heads_width)], axis=1)
    first_pieces = gather_pair_first(first_pack, 0, VAR)
    first_one = jnp.concatenate(first_pieces, axis=0)
    first_two = from_partner(first_one)
    out_block = first_one[:, width:].reshape(half // block, block, heads_width // block, block)
    out_block = out_block.transpose(2, 1, 0, 3).reshape(heads_width, half)
    ring = gather_ring(out_block, TP)
    out_pieces = ring + cross_each(ring, TP)
    down_square = down_weight.reshape(ff_local // block, block, block).transpose(1, 0, 2)
    second_pack = jnp.concatenate(
        [gate_up_weight.reshape(block, 2 * ff_local), down_square.reshape(block, ff_local)], axis=1
    )
    weights = gather_pair_first(second_pack, 0, VAR)
    weights = weights + [from_partner(piece) for piece in weights]

    flat_hidden = hidden_in.reshape(row_count, model_width)
    cosine, sine = rotary_tables(full_len)
    columns = normed_blocks(after(place, cosine, sine), flat_hidden)
    head_rows = attention(columns, first_one, first_two, width, cosine, sine)
    head_rows = head_rows.reshape(tp_count, own_rows, heads_width)

    split = 80
    rest = own_rows - split
    heads = lax.all_to_all(head_rows, "tp", split_axis=0, concat_axis=0, tiled=True)
    other_heads = from_partner(heads)
    one, for_partner = project(place, heads, other_heads, [out_pieces])
    two = from_partner(for_partner)
    after_attention, normed_a, normed_b, switch = combine(
        place, run_flat, tp_flat, one, two, flat_hidden, full_len, split
    )

    other_a = lax.ppermute(normed_a, "tp", TP_XL)
    back_b, ahead_b = send_both(normed_b, TP)
    back_a, ahead_a = send_both(normed_a, TP)
    other_back_a, other_ahead_a = send_both(other_a, TP)
    pair = 2 * split
    for_own, for_pair_a, *joined = first_feed_forward(
        [normed_a, other_a, normed_b],
        [[(0, split), (pair, rest)], [(split, split)]],
        weights,
        ff_local,
    )
    far_a = lax.ppermute(after(back_a, for_pair_a), "tp", TP[2])
    other_far_a = lax.ppermute(after(other_ahead_a, for_pair_a), "tp", TP[3])
    far_b = lax.ppermute(after(back_b, for_pair_a), "tp", TP[2])
    in_a = [normed_a, other_a, back_a, other_back_a, ahead_a, other_ahead_a, far_a, other_far_a]
    in_b = [normed_b, back_b, ahead_b, far_b]
    cross_b = cross_each([normed_b] + [after(t, for_pair_a) for t in in_b[1:]], TP)
    for_back, for_ahead, for_back_pair_a, for_ahead_pair_a = feed_forward(
        in_a[2:6] + in_b[1:3],
        [
            [(0, split), (2 * pair, rest)],
            [(pair, split), (2 * pair + rest, rest)],
            [(split, split)],
            [(pair + split, split)],
        ],
        joined,
    )
    for_far, for_far_pair, for_back_pair_b, for_ahead_pair_b, for_pair_b = feed_forward(
        [in_a[6], in_b[3], in_a[7], cross_b[3], cross_b[1], cross_b[2], cross_b[0]],
        [[(0, own_rows)], [(own_rows, own_rows)]]
        + [[(2 * own_rows + k * rest, rest)] for k in range(3)],
        joined,
    )

    for_far_pair = lax.ppermute(for_far_pair, "tp", TP_XL)
    for_far = (for_far.astype(F32) + for_far_pair.astype(F32)).astype(BF)
    whole_terms = [
        for_own,
        lax.ppermute(for_back, "tp", tp_y(3)),
        lax.ppermute(for_ahead, "tp", tp_y(1)),
        lax.ppermute(for_far, "tp", tp_y(2)),
    ]
    terms_a = [term[:split] for term in whole_terms] + [
        lax.ppermute(for_pair_a, "tp", TP_XL),
        lax.ppermute(for_back_pair_a, "tp", tp_y(3, 1)),
        lax.ppermute(for_ahead_pair_a, "tp", tp_y(1, 1)),
    ]
    terms_b = [term[split:] for term in whole_terms] + [
        lax.ppermute(for_back_pair_b, "tp", tp_y(3, 1)),
        lax.ppermute(for_ahead_pair_b, "tp", tp_y(1, 1)),
        lax.ppermute(for_pair_b, "tp", TP_XL),
    ]

    def finished(rows, terms):
        mlp = sum(term.astype(F32) for term in terms)
        return (after_attention[rows].astype(F32) + switch[rows, :1] * mlp).astype(BF)

    result_a = finished(slice(0, split), terms_a)
    result_b = finished(slice(split, own_rows), terms_b)

    parts_a = gather_each(result_a, TP)
    parts_b = gather_ring(result_b, TP)
    cross = cross_each(parts_b, TP)
    shape = (tp_count, own_rows, model_width)
    pieces = parts_a[:6] + parts_b
    items = [(16 + k, 0) for k in range(6)]
    items += [(24 + k, split) for k in range(4)]
    gathered = place_pieces(place, pieces, items, shape)
    items = [(22, 0), (23, 0)] + [(28 + k, split) for k in range(4)]
    gathered = place_pieces(place, parts_a[6:] + cross, items, shape, gathered)
    return gathered.reshape(seq_count, full_len, model_width)


def solution(mesh):
    return jax.shard_map(
        layer,
        mesh=mesh,
        in_specs=(
            P("var", None, None),
            P("var", None),
            P("var", "tp"),
            P("tp", "var"),
            P("var", None, "tp"),
            P("tp", "var"),
        ),
        out_specs=P("var", None, None),
        check_vma=False,
    )
```
